256 devices in a mesh: grp: 16 (over y, z_lo), blk: 16 (over x, z_hi, core).
Axes of the slice: x: 4, y: 4, z: 8 (z_hi: 2, z_lo: 4; z = z_hi * 4 + z_lo), core: 2. Of those that a mesh axis runs over, the one named last changes fastest.
Arguments:
- front_values: float32 [16384, 16384], P('blk', 'grp'), may hold values from -6 to 6
- diag_scale: float32 [16384], P('blk'), may hold values from 1.5 to 3
- fill_pattern: int32 [128, 128], P('blk', 'grp'), may hold values from 0 to 1, as said below
- supernodes: int32 [2], replicated, may hold values from 0 to 126, as said below
- scenario_loads: float32 [512, 16384], P(('grp', 'blk')), may hold values from -6 to 6
Outputs:
- factored: float32 [16384, 16384], P('blk', 'grp')
- forward_rhs: float32 [512, 16384], P('grp', 'blk')
The draws below stay inside these ranges and needn't reach their ends.
Inputs may be any that keep to these rules, and one draw needn't show every extreme that they name: `fill_pattern`: each entry is 0 or 1; every diagonal block is 1. `supernodes`: two different multiples of 2; the second is always 128 - 2, the last supernode.
All inputs are finite; a program needn't handle non-finite values.
Results may differ from the reference program's by a relative error of at most 0.0001.
Values sent between devices are 32-bit elements; how exact they have to be, the bound alone decides.
A program may use at most 64 MiB of HBM per device.

```python
import math
import jax
import jax.numpy as jnp
from jax import lax

BS = 128
SNB = 2
NS_STEPS = 3
NBLK = 128
N = 16384
SCEN = 512


def draw_fill_pattern(key, part):
    first_key, second_key = jax.random.split(jax.random.fold_in(key, 11))
    density = jax.random.randint(first_key, (NBLK, 1), 10, 95)
    values = jax.random.randint(second_key, (NBLK, NBLK), 0, 100)
    pattern = (values < density).astype(jnp.int32)
    ids = jnp.arange(NBLK, dtype=jnp.int32)
    return jnp.where(ids[:, None] == ids[None, :], 1, pattern).astype(jnp.int32)


def draw_supernodes(key, part):
    picked = jax.random.randint(jax.random.fold_in(key, 23), (1,), 0, NBLK // SNB - 1)
    first = (picked * SNB).astype(jnp.int32)
    last = jnp.full((1,), NBLK - SNB, dtype=jnp.int32)
    return jnp.concatenate([first, last]).astype(jnp.int32)


def levels(key, shape, shards, low, high):
    level, own = 1.0, jax.random.fold_in(key, 6)
    for position, parts in shards:
        draws = jnp.exp(jax.random.uniform(jax.random.fold_in(own, position), (parts,), jnp.float32, low / len(shards), high / len(shards)))
        level = level * jnp.repeat(draws, shape[position] // parts).reshape([-1 if axis == position else 1 for axis in range(len(shape))])
    return level


def gaussian(key, extent, deviation, most, pieces=(), kind=jnp.bfloat16):
    result = deviation * jax.random.normal(key, extent, jnp.float32)
    if pieces:
        result = result * levels(key, extent, pieces, -0.22, 0.18)
    return jnp.clip(result, -most, most).astype(kind)


def setup_inputs(seed: int = 0) -> dict:
    key_of = jax.random.split(jax.random.key(seed), 6)
    return {
        "front_values": gaussian(key_of[0], (N, N), 1.0, 6.0, ((0, 16), (1, 16)), jnp.float32),
        "diag_scale": jnp.clip(1.5 + 1.5 * jax.random.uniform(key_of[1], (N,), jnp.float32) ** levels(key_of[1], (N,), ((0, 16),), -0.2, 0.2), 1.5, 3.0),
        "fill_pattern": draw_fill_pattern(jax.random.fold_in(key_of[5], 71), 0),
        "supernodes": draw_supernodes(jax.random.fold_in(key_of[5], 71), 0),
        "scenario_loads": gaussian(key_of[4], (SCEN, N), 1.0, 6.0, ((0, 256),), jnp.float32),
    }


HIGH = lax.Precision.HIGHEST

def newton_inverse(pivot):
    inverse = jnp.diag(1.0 / jnp.diagonal(pivot))
    for sweep in range(NS_STEPS):
        product = jnp.dot(pivot, inverse, precision=HIGH)
        inverse = 2.0 * inverse - jnp.dot(inverse, product, precision=HIGH)
    return inverse

def reference(front_values, diag_scale, fill_pattern, supernodes, scenario_loads):
    present = jnp.repeat(jnp.repeat(fill_pattern > 0, BS, axis=0), BS, axis=1)
    front = jnp.where(present, front_values, jnp.float32(0.0))
    diag_ids = jnp.arange(N, dtype=jnp.int32)
    front = front.at[diag_ids, diag_ids].add(diag_scale * math.sqrt(N))
    rhs = scenario_loads
    width = SNB * BS
    block_ids = diag_ids // BS
    alive = jnp.ones((N,), dtype=bool)
    for step in range(2):
        first_block = supernodes[step]
        start = (first_block * BS).astype(jnp.int32)
        alive = alive & ~((block_ids >= first_block) & (block_ids < first_block + SNB))
        pivot_rows = lax.dynamic_slice_in_dim(front, start, width, 0)
        pivot_cols = lax.dynamic_slice_in_dim(front, start, width, 1)
        pivot_rhs = lax.dynamic_slice_in_dim(rhs, start, width, 1)
        pivot_block = lax.dynamic_slice_in_dim(pivot_rows, start, width, 1)
        panel = jnp.dot(pivot_cols, newton_inverse(pivot_block), precision=HIGH)
        lower = jnp.where(alive[:, None], panel, jnp.float32(0.0))
        front = lax.dynamic_update_slice_in_dim(front, jnp.where(alive[:, None], panel, pivot_cols), start, 1)
        upper = jnp.where(alive[None, :], pivot_rows, jnp.float32(0.0))
        front = front - jnp.dot(lower, upper, precision=HIGH)
        rhs = rhs - lax.dot_general(pivot_rhs, lower, (((1,), (1,)), ((), ())), precision=HIGH)
    return (front, rhs)
```

```python
import functools
import math

import jax
import jax.numpy as jnp
from jax import lax
from jax.experimental import pallas as pl
from jax.experimental.pallas import tpu as pltpu
from jax.sharding import PartitionSpec as P

MESH = pl.DeviceIdType.MESH
HIGH = lax.Precision.HIGHEST
F32 = jnp.float32
BF16 = jnp.bfloat16

BS = 128
W = 256
NS_STEPS = 3
CH = 16
N = 256 // CH
L = 2
NR = 4
COFF = (0, 1, 1, 2)
SIGN = (1, 1, 3, 3)
LAST = 15


def quarter_of(u, s0, b):
    r0, q0 = s0 // 8, (s0 % 8) // 2
    first = jnp.where(b == r0, q0, jnp.where(b == LAST, 3, 0))
    both = (b == r0) & (b == LAST)

    def swap(v):
        return jnp.where(v == 0, first, jnp.where(v == first, 0, v))

    v = jnp.where(both & (u == 1), 3, jnp.where(both & (u == 3), 1, u))
    return swap(v)


def masked(values, rows, cols, row0, col0, fill_ref, shift, on_diag):
    out = []
    for i in range(rows):
        line = []
        for j in range(cols):
            v = values[i * BS : (i + 1) * BS, j * BS : (j + 1) * BS]
            v = jnp.where(fill_ref[row0 + i, col0 + j] > 0, v, 0.0)
            same = on_diag & (row0 + i == col0 + j)
            r = lax.broadcasted_iota(jnp.int32, (BS, BS), 0)
            c = lax.broadcasted_iota(jnp.int32, (BS, BS), 1)
            d = shift[pl.ds(row0 + i, 1), :]
            v = v + jnp.where((r == c) & same, d, 0.0)
            line.append(v)
        out.append(jnp.concatenate(line, axis=1) if cols > 1 else line[0])
    return jnp.concatenate(out, axis=0) if rows > 1 else out[0]


def prep_kernel(sc, fill, front, top0, top1, shift, loads, cbuf, rbuf, piv):
    u = pl.program_id(0)
    s0, g, b = sc[0], sc[2], sc[3]
    q0 = (s0 % 8) // 2
    aq = quarter_of(u, s0, b)
    diag = g == b
    for k, q in ((0, q0), (1, 3)):
        v = front[:, pl.ds(pl.multiple_of(q * W, W), W)]
        v = masked(v, 2, 2, aq * 2, q * 2, fill, shift, diag)
        cbuf[k] = v.reshape(4, 64, W)
        t = (top0, top1)[k][...]
        rbuf[k] = masked(t, 2, 2, q * 2, u * 2, fill, shift, diag)
    piv[:, 0:W] = loads[:, pl.ds(pl.multiple_of(s0 * BS, W), W)]
    piv[:, W : 2 * W] = loads[:, loads.shape[1] - W :]


def comm_kernel(r0, cin, rin, loads, piv, cbuf, rbuf, dbuf, hbuf, pbuf,
                cs, cr, rs, rown, roth, dsem, down, doth, hs, hr, loc):
    g, b = lax.axis_index("grp"), lax.axis_index("blk")
    y, zl = g // 4, g % 4
    x, zh, c = b // 4, (b // 2) % 2, b % 2
    partner = {"blk": x * 4 + zh * 2 + (1 - c)}

    barrier = pltpu.get_barrier_semaphore()

    @pl.loop(1, 16)
    def _(i):
        pl.semaphore_signal(barrier, inc=1, device_id={"blk": (b + i) % 16}, device_id_type=MESH)

    for t in (((y + 1) % 4) * 4 + zl, ((y + 3) % 4) * 4 + zl, y * 4 + (zl + 1) % 4, y * 4 + (zl + 3) % 4):
        pl.semaphore_signal(barrier, inc=1, device_id={"grp": t}, device_id_type=MESH)
    pl.semaphore_wait(barrier, 19)

    def rdma(src, dst, ssem, rsem, to):
        return pltpu.make_async_remote_copy(
            src_ref=src, dst_ref=dst, send_sem=ssem, recv_sem=rsem, device_id=to, device_id_type=MESH)

    roots = (r0, LAST)
    place = (0, 1 if r0 == LAST else 0)

    cplan = []
    for k in range(2):
        yk, zk = roots[k] // 4, roots[k] % 4
        inplane = zl == zk
        e = jnp.where(zl > zk, zl - zk, zk - zl)
        for cls in range(4):
            a = ((y + 4 - yk) * SIGN[cls]) % 4
            eff = jnp.where(inplane, a, (a + 4 - COFF[cls]) % 4)
            lag = jnp.where(inplane, a, COFF[cls] + e + eff) * L
            at = a == COFF[cls]
            cplan.append(dict(
                k=k, cls=cls, lag=lag, root=inplane & (a == 0), ring=eff != 3,
                up=at & (zl >= zk) & (zl < 3), dn=at & (zl <= zk) & (zl > 0),
                ringto={"grp": ((y + SIGN[cls]) % 4) * 4 + zl},
                upto={"grp": y * 4 + jnp.minimum(zl + 1, 3)}, dnto={"grp": y * 4 + jnp.maximum(zl - 1, 0)}))
    rplan = []
    for k in range(2):
        xk, hk, ck = roots[k] // 4, (roots[k] // 2) % 2, roots[k] % 2
        inhalf = zh == hk
        for cls in range(4):
            a = ((x + 4 - xk) * SIGN[cls]) % 4
            eff = jnp.where(inhalf, a, (a + 4 - COFF[cls]) % 4)
            lag = jnp.where(inhalf, a, COFF[cls] + 2 + eff) * L + jnp.where(c == ck, 0, L)
            chip = inhalf & (x == xk)
            rplan.append(dict(
                k=k, cls=cls, lag=lag, root=chip & (c == ck), mate=chip & (c != ck), ring=eff != 3,
                cross=inhalf & (a == COFF[cls]),
                ringto={"blk": ((x + SIGN[cls]) % 4) * 4 + zh * 2 + c},
                crossto={"blk": x * 4 + (1 - zh) * 2 + c}))
    tds = [(place[k] + 1) * (64 // CH) + 8 * L for k in range(2)]
    turns = max(N + 8 * L, max(tds) + 2 + 9 * L)

    @pl.loop(1, 16)
    def _(i):
        to = (b + i) % 16
        cols = pl.ds(pl.multiple_of(to * 1024, 1024), 1024)
        rdma(loads.at[:, cols], hbuf.at[b], hs.at[0], hr.at[0, i], {"blk": to}).start()
        rdma(piv, pbuf.at[b], hs.at[1], hr.at[1, i], {"blk": to}).start()

    mine = [
        pltpu.make_async_copy(loads.at[:, pl.ds(pl.multiple_of(b * 1024, 1024), 1024)], hbuf.at[b], loc.at[0]),
        pltpu.make_async_copy(piv, pbuf.at[b], loc.at[1]),
    ]
    for m in mine:
        m.start()

    def dlocal(k):
        lo = place[k] * 64
        return pltpu.make_async_copy(cbuf.at[:, :, pl.ds(lo, 64), :], dbuf.at[k], loc.at[2 + k])

    @pl.loop(0, turns)
    def _(t):
        for p in cplan:
            k, cls = p["k"], p["cls"]
            n = t - p["lag"]

            @pl.when((n >= 0) & (n < N))
            def _():
                rows = cbuf.at[k, cls, pl.ds(pl.multiple_of(n * CH, CH), CH), :]
                sem = cr.at[k, cls, n]

                @pl.when(jnp.logical_not(p["root"]))
                def _():
                    rdma(rows, rows, cs.at[0, k, cls], sem, p["ringto"]).wait_recv()

                for i, (on, to) in enumerate((("ring", "ringto"), ("up", "upto"), ("dn", "dnto"))):
                    @pl.when(p[on])
                    def _():
                        rdma(rows, rows, cs.at[i, k, cls], sem, p[to]).start()

        for p in rplan:
            k, cls = p["k"], p["cls"]
            n = t - p["lag"]

            @pl.when((n >= 0) & (n < NR))
            def _():
                rows = rbuf.at[k, c, cls, pl.ds(pl.multiple_of(n * 8, 8), 8), :]

                @pl.when(jnp.logical_not(p["root"]))
                def _():
                    rdma(rows, rows, rs.at[0, k, cls], rown.at[k, cls, n], p["ringto"]).wait_recv()

                for i, (on, to) in enumerate((("ring", "ringto"), ("cross", "crossto"))):
                    @pl.when(p[on])
                    def _():
                        rdma(rows, rows, rs.at[i, k, cls], rown.at[k, cls, n], p[to]).start()

                @pl.when(jnp.logical_not(p["mate"]))
                def _():
                    rdma(rows, rows, rs.at[2, k, cls], roth.at[k, cls, n], partner).start()

                @pl.when(p["root"])
                def _():
                    other = rbuf.at[k, 1 - c, cls, pl.ds(pl.multiple_of(n * 8, 8), 8), :]
                    rdma(other, other, rs.at[3, k, cls], rown.at[k, cls, n], partner).start()

            j = n - tds[k]

            @pl.when((j >= 0) & (j < 2))
            def _():
                part = pl.ds(pl.multiple_of(c * 32, 32), 32)
                dst = dbuf.at[k, j, cls, part, :]
                sem = down.at[k, cls, j]

                @pl.when(p["root"])
                def _():
                    lo = place[k] * 64
                    src = cbuf.at[j, cls, pl.ds(pl.multiple_of(lo + c * 32, 32), 32), :]
                    for i, (on, to) in enumerate((("ring", "ringto"), ("cross", "crossto"))):
                        @pl.when(p[on])
                        def _():
                            rdma(src, dst, dsem.at[i, k, cls], sem, p[to]).start()

                    rdma(src, dst, dsem.at[2, k, cls], doth.at[k, cls, j], partner).start()
                    src2 = cbuf.at[j, cls, pl.ds(pl.multiple_of(lo + (1 - c) * 32, 32), 32), :]
                    dst2 = dbuf.at[k, j, cls, pl.ds(pl.multiple_of((1 - c) * 32, 32), 32), :]
                    rdma(src2, dst2, dsem.at[3, k, cls], sem, partner).start()

                @pl.when(jnp.logical_not(p["root"]))
                def _():
                    rdma(dst, dst, dsem.at[0, k, cls], sem, p["ringto"]).wait_recv()
                    for i, (on, to) in enumerate((("ring", "ringto"), ("cross", "crossto"))):
                        @pl.when(p[on])
                        def _():
                            rdma(dst, dst, dsem.at[i, k, cls], sem, p[to]).start()

                    @pl.when(jnp.logical_not(p["mate"]))
                    def _():
                        rdma(dst, dst, dsem.at[2, k, cls], doth.at[k, cls, j], partner).start()

        for k in range(2):
            @pl.when((t == tds[k]) & (b == roots[k]))
            def _():
                dlocal(k).start()

    for p in rplan:
        k, cls = p["k"], p["cls"]

        @pl.when(jnp.logical_not(p["root"]))
        def _():
            @pl.loop(0, NR)
            def _(n):
                rows = rbuf.at[k, 1 - c, cls, pl.ds(pl.multiple_of(n * 8, 8), 8), :]
                rdma(rows, rows, rs.at[2, k, cls], roth.at[k, cls, n], partner).wait_recv()

            @pl.loop(0, 2)
            def _(j):
                rows = dbuf.at[k, j, cls, pl.ds(pl.multiple_of((1 - c) * 32, 32), 32), :]
                rdma(rows, rows, dsem.at[2, k, cls], doth.at[k, cls, j], partner).wait_recv()

    @pl.loop(1, 16)
    def _(i):
        rdma(piv, pbuf.at[b], hs.at[1], hr.at[1, i], partner).wait_recv()
        rdma(hbuf.at[b], hbuf.at[b], hs.at[0], hr.at[0, i], partner).wait_recv()

    for p in cplan:
        k, cls = p["k"], p["cls"]
        for i, on in enumerate(("ring", "up", "dn")):
            @pl.when(p[on])
            def _():
                rdma(cbuf.at[k, cls], cbuf.at[k, cls], cs.at[i, k, cls], cr.at[k, cls, 0], p["ringto"]).wait_send()
    for p in rplan:
        k, cls = p["k"], p["cls"]
        half = rbuf.at[k, c, cls]
        dhalf = dbuf.at[k, :, cls, pl.ds(pl.multiple_of(c * 32, 32), 32), :]
        for i, on in enumerate((p["ring"], p["cross"], jnp.logical_not(p["mate"]), p["root"])):
            @pl.when(on)
            def _():
                rdma(half, half, rs.at[i, k, cls], rown.at[k, cls, 0], p["ringto"]).wait_send()
                rdma(dhalf, dhalf, dsem.at[i, k, cls], down.at[k, cls, 0], p["ringto"]).wait_send()
    for m in mine:
        m.wait()
    for k in range(2):
        @pl.when(b == roots[k])
        def _():
            dlocal(k).wait()

    @pl.loop(1, 16)
    def _(i):
        rdma(hbuf.at[b], hbuf.at[b], hs.at[0], hr.at[0, i], partner).wait_send()
        rdma(piv, pbuf.at[b], hs.at[1], hr.at[1, i], partner).wait_send()


def comm(r0, cbuf, rbuf, loads, piv):
    anyspec = pl.BlockSpec(memory_space=pl.ANY)
    dma = pltpu.SemaphoreType.DMA
    return pl.pallas_call(
        functools.partial(comm_kernel, r0),
        out_shape=(
            jax.ShapeDtypeStruct(cbuf.shape, F32),
            jax.ShapeDtypeStruct(rbuf.shape, F32),
            jax.ShapeDtypeStruct((2, 2, 4, 64, W), F32),
            jax.ShapeDtypeStruct((16, 2, 1024), F32),
            jax.ShapeDtypeStruct((16, 2, 2 * W), F32),
        ),
        in_specs=[anyspec] * 4,
        out_specs=(anyspec,) * 5,
        input_output_aliases={0: 0, 1: 1},
        scratch_shapes=[
            dma((3, 2, 4)), dma((2, 4, N)),
            dma((4, 2, 4)), dma((2, 4, NR)), dma((2, 4, NR)),
            dma((4, 2, 4)), dma((2, 4, 2)), dma((2, 4, 2)),
            dma((2,)), dma((2, 16)), dma((4,)),
        ],
        compiler_params=pltpu.CompilerParams(collective_id=r0, has_side_effects=True),
        name="exchange_%d" % r0,
    )(cbuf, rbuf, loads, piv)


def split(v):
    hi = v.astype(BF16)
    return hi, (v - hi.astype(F32)).astype(BF16)


def mm(a, b):
    return jnp.dot(a, b, preferred_element_type=F32)


def mm3(a, b):
    return mm(a[0], b[0]) + (mm(a[0], b[1]) + mm(a[1], b[0]))


def mm3t(a, b):
    dims = (((1,), (1,)), ((), ()))

    def one(p, q):
        return lax.dot_general(p, q, dims, preferred_element_type=F32)

    return one(a[0], b[0]) + (one(a[0], b[1]) + one(a[1], b[0]))


def full(a, b):
    return jnp.dot(a, b, precision=HIGH, preferred_element_type=F32)


def newton(pivot):
    n = pivot.shape[0]
    r = lax.broadcasted_iota(jnp.int32, (n, n), 0)
    c = lax.broadcasted_iota(jnp.int32, (n, n), 1)
    eye = r == c
    kept = jnp.where(eye, pivot, 0.0)
    drow = 1.0 / jnp.sum(kept, axis=0, keepdims=True)
    dcol = 1.0 / jnp.sum(kept, axis=1, keepdims=True)
    inv = jnp.where(eye, 2.0 * drow, 0.0) - dcol * (pivot * drow)
    for _ in range(NS_STEPS - 1):
        inv = 2.0 * inv - full(inv, full(pivot, inv))
    return inv


def update_kernel(sc, fill, front, shift, cbuf, rbuf, dbuf, hbuf, pbuf, out, hout,
                  x0h, x0l, x1h, x1l, d1h, d1l, uh, ul, pvh, pvl):
    u = pl.program_id(0)
    s0, g, b = sc[0], sc[2], sc[3]
    r0, q0 = s0 // 8, (s0 % 8) // 2
    cols = front.shape[1]
    ids = lax.broadcasted_iota(jnp.int32, (1, cols), 1) // W
    dead0 = (g == r0) & (ids == q0)
    dead1 = (g == LAST) & (ids == 3)

    @pl.when(u == 0)
    def _():
        d = [[dbuf[i, j].reshape(W, W) for j in range(2)] for i in range(2)]
        x0 = newton(d[0][0])
        m = full(d[1][0], x0)
        x1 = newton(d[1][1] - full(m, d[0][1]))
        x0h[...], x0l[...] = split(x0)
        x1h[...], x1l[...] = split(x1)
        d1h[...], d1l[...] = split(d[0][1])
        ms = split(m)
        u0 = jnp.where(dead0, 0.0, rbuf[0])
        u0s = split(u0)
        u1 = jnp.where(dead0 | dead1, 0.0, rbuf[1] - mm3(ms, u0s))
        u1s = split(u1)
        uh[0:W], ul[0:W] = u0s
        uh[W : 2 * W], ul[W : 2 * W] = u1s
        pv = jnp.concatenate([pbuf[:, 0, :], pbuf[:, 1, :]], axis=0)
        p0 = split(pv[:, 0:W])
        p1 = split(pv[:, W : 2 * W] - mm3t(p0, ms))
        pvh[:, 0:W], pvl[:, 0:W] = p0
        pvh[:, W : 2 * W], pvl[:, W : 2 * W] = p1

    aq = quarter_of(u, s0, b)
    gone0 = (b == r0) & (aq == q0)
    gone1 = (b == LAST) & (aq == 3)
    c0 = cbuf[0].reshape(W, W)
    l0 = mm3(split(c0), (x0h[...], x0l[...]))
    l0 = jnp.where(gone0, 0.0, l0)
    l0s = split(l0)
    c1 = cbuf[1].reshape(W, W) - mm3(l0s, (d1h[...], d1l[...]))
    l1 = mm3(split(c1), (x1h[...], x1l[...]))
    l1 = jnp.where(gone0 | gone1, 0.0, l1)
    l1s = split(l1)
    lh = jnp.concatenate([l0s[0], l1s[0]], axis=1)
    ll = jnp.concatenate([l0s[1], l1s[1]], axis=1)
    for j in range(cols // W):
        sl = slice(j * W, (j + 1) * W)
        f = masked(front[:, sl], 2, 2, aq * 2, j * 2, fill, shift, g == b)
        f = f - mm3((lh, ll), (uh[:, sl], ul[:, sl]))
        f = jnp.where((g == r0) & (q0 == j) & jnp.logical_not(gone0), l0, f)
        if j == 3:
            f = jnp.where(g == LAST, jnp.where(gone0 | gone1, c1, l1), f)
        out[:, sl] = f
    here = pl.ds(pl.multiple_of(aq * W, W), W)
    h = jnp.concatenate([hbuf[:, 0, here], hbuf[:, 1, here]], axis=0)
    h = h - mm3t((pvh[...], pvl[...]), (lh, ll))
    hout[0, :, here] = h[0:16]
    hout[1, :, here] = h[16:32]


def per_device(front, diag, fill, supernodes, loads):
    rows, cols = front.shape
    order = rows * lax.axis_size("blk")
    g, b = lax.axis_index("grp"), lax.axis_index("blk")
    sc = jnp.stack([supernodes[0], supernodes[1], g, b]).astype(jnp.int32)
    shift = (diag * math.sqrt(order)).reshape(rows // BS, BS)
    smem = pl.BlockSpec(memory_space=pltpu.SMEM)

    def const(shape):
        return pl.BlockSpec(shape, lambda u, sc: (0,) * len(shape))

    cbuf, rbuf, piv = pl.pallas_call(
        prep_kernel,
        out_shape=(
            jax.ShapeDtypeStruct((2, 4, 256, W), F32),
            jax.ShapeDtypeStruct((2, W, cols), F32),
            jax.ShapeDtypeStruct((2, 2 * W), F32),
        ),
        grid_spec=pltpu.PrefetchScalarGridSpec(
            num_scalar_prefetch=1,
            grid=(4,),
            in_specs=[
                smem,
                pl.BlockSpec((W, cols), lambda u, sc: (quarter_of(u, sc[0], sc[3]), 0)),
                pl.BlockSpec((W, W), lambda u, sc: ((sc[0] % 8) // 2, u)),
                pl.BlockSpec((W, W), lambda u, sc: (3, u)),
                const(shift.shape),
                const(loads.shape),
            ],
            out_specs=(
                pl.BlockSpec((2, 4, 64, W), lambda u, sc: (0, 0, u, 0)),
                pl.BlockSpec((2, W, W), lambda u, sc: (0, 0, u)),
                const((2, 2 * W)),
            ),
        ),
        name="panels",
    )(sc, fill, front, front, front, shift, loads)
    rbuf = rbuf.reshape(2, 2, 4, 32, cols)
    cbuf, rbuf, dbuf, hbuf, pbuf = lax.switch(
        supernodes[0] // 8, [functools.partial(comm, r) for r in range(16)], cbuf, rbuf, loads, piv)
    rbuf = rbuf.reshape(2, W, cols)
    out, hout = pl.pallas_call(
        update_kernel,
        out_shape=(
            jax.ShapeDtypeStruct((rows, cols), F32),
            jax.ShapeDtypeStruct((2, 16, rows), F32),
        ),
        grid_spec=pltpu.PrefetchScalarGridSpec(
            num_scalar_prefetch=1,
            grid=(4,),
            in_specs=[
                smem,
                pl.BlockSpec((W, cols), lambda u, sc: (quarter_of(u, sc[0], sc[3]), 0)),
                const(shift.shape),
                pl.BlockSpec((2, 4, 64, W), lambda u, sc: (0, 0, u, 0)),
                const(rbuf.shape),
                const(dbuf.shape),
                const(hbuf.shape),
                const(pbuf.shape),
            ],
            out_specs=(
                pl.BlockSpec((W, cols), lambda u, sc: (quarter_of(u, sc[0], sc[3]), 0)),
                const((2, 16, rows)),
            ),
            scratch_shapes=[pltpu.VMEM((W, W), BF16)] * 6
            + [pltpu.VMEM((2 * W, cols), BF16)] * 2
            + [pltpu.VMEM((32, 2 * W), BF16)] * 2,
        ),
        name="update",
    )(sc, fill, front, shift, cbuf, rbuf, dbuf, hbuf, pbuf)
    return out, jnp.swapaxes(hout, 0, 1).reshape(32, rows)


def solution(mesh):
    in_specs = (P("blk", "grp"), P("blk"), P("blk", "grp"), P(), P(("grp", "blk"), None))
    out_specs = (P("blk", "grp"), P("grp", "blk"))
    return jax.shard_map(
        per_device, mesh=mesh, in_specs=in_specs, out_specs=out_specs, check_vma=False
    )
```

```python
import functools
import math

import jax
import jax.numpy as jnp
from jax import lax
from jax.experimental import pallas as pl
from jax.experimental.pallas import tpu as pltpu
from jax.sharding import PartitionSpec as P

MESH = pl.DeviceIdType.MESH
HIGH = lax.Precision.HIGHEST
F32 = jnp.float32
BF16 = jnp.bfloat16

BS = 128
W = 256
NS_STEPS = 3
CH = 32
N = 256 // CH
LG = 1
NR = 4
LAST = 15


def quarter_of(u, s0, b):
    r0, q0 = s0 // 8, (s0 % 8) // 2
    first = jnp.where(b == r0, q0, jnp.where(b == LAST, 3, 0))
    both = (b == r0) & (b == LAST)

    def swap(v):
        return jnp.where(v == 0, first, jnp.where(v == first, 0, v))

    v = jnp.where(both & (u == 1), 3, jnp.where(both & (u == 3), 1, u))
    return swap(v)


def masked(weight, values, rows, cols, row0, col0, fill_ref, shift, on_diag):
    out = []
    for i in range(rows):
        line = []
        for j in range(cols):
            v = values[i * BS : (i + 1) * BS, j * BS : (j + 1) * BS]
            v = jnp.where(fill_ref[row0 + i, col0 + j] > 0, v, 0.0)
            same = on_diag & (row0 + i == col0 + j)
            r = lax.broadcasted_iota(jnp.int32, (BS, BS), 0)
            c = lax.broadcasted_iota(jnp.int32, (BS, BS), 1)
            d = shift[pl.ds(row0 + i, 1), :] * weight
            v = v + jnp.where((r == c) & same, d, 0.0)
            line.append(v)
        out.append(jnp.concatenate(line, axis=1) if cols > 1 else line[0])
    return jnp.concatenate(out, axis=0) if rows > 1 else out[0]


def prep_kernel(weight, sc, fill, front, top0, top1, shift, loads, cbuf, rbuf, piv):
    u = pl.program_id(0)
    s0, g, b = sc[0], lax.axis_index("grp"), lax.axis_index("blk")
    q0 = (s0 % 8) // 2
    aq = quarter_of(u, s0, b)
    diag = g == b
    for k, q in ((0, q0), (1, 3)):
        v = front[:, pl.ds(pl.multiple_of(q * W, W), W)]
        v = masked(weight, v, 2, 2, aq * 2, q * 2, fill, shift, diag)
        cbuf[k] = v.reshape(4, 64, W)
        t = (top0, top1)[k][...]
        rbuf[k] = masked(weight, t, 2, 2, q * 2, u * 2, fill, shift, diag)
    piv[:, 0:W] = loads[:, pl.ds(pl.multiple_of(s0 * BS, W), W)]
    piv[:, W : 2 * W] = loads[:, loads.shape[1] - W :]


def comm_kernel(r0, cin, rin, loads, piv, cbuf, rbuf, dbuf, hbuf, pbuf,
                cs, cz, cr, rs, rx, rown, roth, ds, dx, down, doth, hs, hr, loc):
    g, b = lax.axis_index("grp"), lax.axis_index("blk")
    y, zl = g // 4, g % 4
    x, zh, c = b // 4, (b // 2) % 2, b % 2
    partner = {"blk": x * 4 + zh * 2 + (1 - c)}
    cross = {"blk": x * 4 + (1 - zh) * 2 + c}

    def xto(i):
        return {"blk": ((x + i) % 4) * 4 + zh * 2 + c}

    def yto(i):
        return {"grp": ((y + i) % 4) * 4 + zl}

    def zto(i):
        return {"grp": y * 4 + i}

    barrier = pltpu.get_barrier_semaphore()

    @pl.loop(1, 16)
    def _(i):
        pl.semaphore_signal(barrier, inc=1, device_id={"blk": (b + i) % 16}, device_id_type=MESH)

    @pl.loop(1, 4)
    def _(i):
        pl.semaphore_signal(barrier, inc=1, device_id=yto(i), device_id_type=MESH)
        pl.semaphore_signal(barrier, inc=1, device_id=zto((zl + i) % 4), device_id_type=MESH)

    pl.semaphore_wait(barrier, 21)

    def rdma(src, dst, ssem, rsem, to):
        return pltpu.make_async_remote_copy(
            src_ref=src, dst_ref=dst, send_sem=ssem, recv_sem=rsem, device_id=to, device_id_type=MESH)

    nots = jnp.logical_not
    place = (0, 1 if r0 == LAST else 0)

    def pick(k, first, second):
        return jnp.where(k == 0, first, second)

    def way(cls):
        return jnp.where(cls < 2, 1, 3), jnp.where(cls < 2, 3, 1)

    def ring(pos, root):
        a = (pos + 4 - root) % 4
        own = jnp.where(a == 3, 2, jnp.where(a == 2, 3, a))
        return a, own, jnp.where(a == 3, 1, a)

    def cplan(k):
        yk, zk = pick(k, r0 // 4, LAST // 4), pick(k, r0 % 4, LAST % 4)
        a, own, hop = ring(y, yk)
        e = jnp.where(zl > zk, zl - zk, zk - zl)
        lag = (hop + jnp.where(e == 0, 0, jnp.where(e == 3, 2, 1))) * LG
        return a, own, e == 0, lag, zk

    def rplan(k):
        xk, hk, ck = pick(k, r0 // 4, 3), pick(k, (r0 // 2) % 2, 1), pick(k, r0 % 2, 1)
        a, own, hop = ring(x, xk)
        inside = zh == hk
        lag = (hop + jnp.where(inside, 0, 2) + jnp.where(c == ck, 0, 1)) * LG
        return a, own, inside, lag, inside & (a == 0) & (c == ck), inside & (a == 0) & (c != ck)

    def waits(a, own, inside, origin, cls):
        return jnp.where(inside, nots(origin) & (a == way(cls)[1]), cls != own)

    def crow(k, cls, n):
        return cbuf.at[k, cls, pl.ds(pl.multiple_of(n * CH, CH), CH), :]

    def csend(k, cls, n, sem, to):
        rdma(crow(k, cls, n), crow(k, cls, n), sem, cr.at[k, cls, n], to).start()

    def cwait(k, cls, n):
        rdma(crow(k, cls, n), crow(k, cls, n), cs.at[k, 0], cr.at[k, cls, n], yto(1)).wait_recv()

    def rrow(k, half, cls, n):
        return rbuf.at[k, half, cls, pl.ds(pl.multiple_of(n * 8, 8), 8), :]

    def rsend(k, half, cls, n, sem, to):
        rdma(rrow(k, half, cls, n), rrow(k, half, cls, n), sem, rown.at[k, cls, n], to).start()

    def rwait(k, cls, n):
        rdma(rrow(k, c, cls, n), rrow(k, c, cls, n), rs.at[k, 0], rown.at[k, cls, n], xto(1)).wait_recv()

    def drow(k, cls, half):
        return dbuf.at[k, :, cls, pl.ds(pl.multiple_of(half * 32, 32), 32), :]

    def dsource(k, cls, half):
        at = pl.multiple_of(pick(k, place[0], place[1]) * 64 + half * 32, 32)
        return cbuf.at[:, cls, pl.ds(at, 32), :]

    def dsend(k, cls, sem, to):
        rdma(drow(k, cls, c), drow(k, cls, c), sem, down.at[k, cls], to).start()

    def dwait(k, cls):
        rdma(drow(k, cls, c), drow(k, cls, c), ds.at[k, 0], down.at[k, cls], xto(1)).wait_recv()

    early = [(p + 1) * (64 // CH) for p in place]
    tds = [4 * LG + e - 1 for e in early]
    turns = max(N + 4 * LG, max(tds) + 1 + 5 * LG)

    def cfinal(lo, hi):
        @pl.loop(0, 2)
        def _(k):
            a, own, inside, lag, zk = cplan(k)

            @pl.loop(0, 4)
            def _(cls):
                @pl.when(waits(a, own, inside, a == 0, cls))
                def _():
                    @pl.loop(lo, hi)
                    def _(n):
                        cwait(k, cls, n)

    def mine(k):
        return pltpu.make_async_copy(cbuf.at[:, :, pl.ds(place[k] * 64, 64), :], dbuf.at[k], loc.at[2 + k])

    own_h = [
        pltpu.make_async_copy(loads.at[:, pl.ds(pl.multiple_of(b * 1024, 1024), 1024)], hbuf.at[b], loc.at[0]),
        pltpu.make_async_copy(piv, pbuf.at[b], loc.at[1]),
    ]

    @pl.loop(0, turns)
    def _(t):
        @pl.loop(0, 2)
        def _(k):
            a, own, inside, lag, zk = cplan(k)
            n = t - lag
            on = (n >= 0) & (n < N)

            @pl.when(on & inside)
            def _():
                @pl.loop(0, 4)
                def _(cls):
                    step, end = way(cls)

                    @pl.when(a != end)
                    def _():
                        @pl.when(a != 0)
                        def _():
                            cwait(k, cls, n)

                        csend(k, cls, n, cs.at[k, cls], yto(step))

                @pl.loop(0, 4)
                def _(z):
                    @pl.when((z != zl) & (z - zl < 3) & (zl - z < 3))
                    def _():
                        csend(k, own, n, cz.at[k, z], zto(z))

            @pl.when(on & nots(inside))
            def _():
                cwait(k, own, n)

                @pl.when(((zk == 0) & (zl == 2)) | ((zk == 3) & (zl == 1)))
                def _():
                    csend(k, own, n, cz.at[k, 0], zto(3 - zk))

                @pl.loop(1, 4)
                def _(i):
                    j = jnp.where(i == 1, 2, jnp.where(i == 2, 1, 3))
                    csend(k, own, n, cs.at[k, j], yto(j))

            a, own, inside, lag, root, mate = rplan(k)
            n = t - lag
            on = (n >= 0) & (n < NR)

            @pl.when(on & inside)
            def _():
                @pl.loop(0, 4)
                def _(cls):
                    step, end = way(cls)

                    @pl.when(root)
                    def _():
                        rsend(k, 1 - c, cls, n, rx.at[k, 1], partner)

                    @pl.when(a != end)
                    def _():
                        @pl.when(nots(root))
                        def _():
                            rwait(k, cls, n)

                        rsend(k, c, cls, n, rs.at[k, cls], xto(step))

                rsend(k, c, own, n, rx.at[k, 0], cross)

            @pl.when(on & nots(inside))
            def _():
                rwait(k, own, n)

                @pl.loop(1, 4)
                def _(i):
                    j = jnp.where(i == 1, 2, jnp.where(i == 2, 1, 3))
                    rsend(k, c, own, n, rs.at[k, j], xto(j))

        @pl.when(t == 2)
        def _():
            for m in own_h:
                m.start()

            @pl.loop(1, 16)
            def _(i):
                to = (b + i) % 16
                cols = pl.ds(pl.multiple_of(to * 1024, 1024), 1024)
                rdma(loads.at[:, cols], hbuf.at[b], hs.at[0], hr.at[0, i], {"blk": to}).start()
                rdma(piv, pbuf.at[b], hs.at[1], hr.at[1, i], {"blk": to}).start()

        for i, td in enumerate(sorted(set(tds))):
            @pl.when(t == td)
            def _():
                cfinal(0 if i == 0 else early[0], td - 4 * LG + 1)
                for k in range(2):
                    if tds[k] == td:
                        @pl.when(b == (r0, LAST)[k])
                        def _():
                            mine(k).start()

        @pl.loop(0, 2)
        def _(k):
            a, own, inside, lag, root, mate = rplan(k)
            on = t - lag == pick(k, tds[0], tds[1])

            @pl.when(on & inside)
            def _():
                @pl.loop(0, 4)
                def _(cls):
                    step, end = way(cls)

                    @pl.when(root)
                    def _():
                        rdma(dsource(k, cls, 1 - c), drow(k, cls, 1 - c), dx.at[k, 1], down.at[k, cls],
                             partner).start()
                        rdma(dsource(k, cls, c), drow(k, cls, c), ds.at[k, cls], down.at[k, cls],
                             xto(step)).start()

                    @pl.when(nots(root) & (a != end))
                    def _():
                        dwait(k, cls)
                        dsend(k, cls, ds.at[k, cls], xto(step))

                @pl.when(root)
                def _():
                    rdma(dsource(k, 0, c), drow(k, 0, c), dx.at[k, 0], down.at[k, 0], cross).start()

                    @pl.loop(0, 4)
                    def _(cls):
                        rdma(dsource(k, cls, c), drow(k, cls, c), dx.at[k, 2], doth.at[k, cls], partner).start()

                @pl.when(nots(root))
                def _():
                    dsend(k, own, dx.at[k, 0], cross)

            @pl.when(on & nots(inside))
            def _():
                dwait(k, own)

                @pl.loop(1, 4)
                def _(i):
                    j = jnp.where(i == 1, 2, jnp.where(i == 2, 1, 3))
                    dsend(k, own, ds.at[k, j], xto(j))

    @pl.loop(0, 2)
    def _(k):
        a, own, inside, lag, root, mate = rplan(k)

        @pl.loop(0, 4)
        def _(cls):
            @pl.when(waits(a, own, inside, a == 0, cls))
            def _():
                @pl.loop(0, NR)
                def _(n):
                    rwait(k, cls, n)

            @pl.when(nots(mate))
            def _():
                half = rbuf.at[k, c, cls]
                rdma(half, half, rx.at[k, 2], roth.at[k, cls], partner).start()

    @pl.loop(0, 2)
    def _(k):
        a, own, inside, lag, root, mate = rplan(k)

        @pl.loop(0, 4)
        def _(cls):
            @pl.when(waits(a, own, inside, a == 0, cls))
            def _():
                dwait(k, cls)

            @pl.when(nots(mate | root))
            def _():
                rdma(drow(k, cls, c), drow(k, cls, c), dx.at[k, 2], doth.at[k, cls], partner).start()

    cfinal(max(early), N)

    @pl.loop(1, 16)
    def _(i):
        rdma(piv, pbuf.at[b], hs.at[1], hr.at[1, i], partner).wait_recv()
        rdma(hbuf.at[b], hbuf.at[b], hs.at[0], hr.at[0, i], partner).wait_recv()

    @pl.loop(0, 2)
    def _(k):
        a, own, inside, lag, root, mate = rplan(k)

        @pl.when(nots(root))
        def _():
            @pl.loop(0, 4)
            def _(cls):
                rest = rbuf.at[k, 1 - c, cls]
                rdma(rest, rest, rx.at[k, 2], roth.at[k, cls], partner).wait_recv()
                part = drow(k, cls, 1 - c)
                rdma(part, part, dx.at[k, 2], doth.at[k, cls], partner).wait_recv()

    @pl.loop(0, 2)
    def _(k):
        ca, cown, cin_, clag, zk = cplan(k)
        a, own, inside, lag, root, mate = rplan(k)

        def csent(sem):
            rdma(cbuf.at[k, 0], cbuf.at[k, 0], sem, cr.at[k, 0, 0], yto(1)).wait_send()

        def rsent(sem):
            rdma(rbuf.at[k, c, 0], rbuf.at[k, c, 0], sem, rown.at[k, 0, 0], xto(1)).wait_send()

        def dsent(sem):
            rdma(drow(k, 0, c), drow(k, 0, c), sem, down.at[k, 0], xto(1)).wait_send()

        @pl.loop(0, 4)
        def _(i):
            @pl.when(jnp.where(cin_, ca != way(i)[1], i > 0))
            def _():
                csent(cs.at[k, i])

            @pl.when(jnp.where(inside, a != way(i)[1], i > 0))
            def _():
                rsent(rs.at[k, i])
                dsent(ds.at[k, i])

            far = (i == 0) & (((zk == 0) & (zl == 2)) | ((zk == 3) & (zl == 1)))

            @pl.when(jnp.where(cin_, (i != zl) & (i - zl < 3) & (zl - i < 3), far))
            def _():
                csent(cz.at[k, i])

        @pl.when(inside)
        def _():
            rsent(rx.at[k, 0])
            dsent(dx.at[k, 0])

        def whole(sem, dsem):
            rdma(rbuf.at[k, 0], rbuf.at[k, 0], sem, rown.at[k, 0, 0], xto(1)).wait_send()
            part = dbuf.at[k, :, :, 0:32, :]
            rdma(part, part, dsem, down.at[k, 0], xto(1)).wait_send()

        @pl.when(root)
        def _():
            whole(rx.at[k, 1], dx.at[k, 1])

        @pl.when(nots(mate))
        def _():
            whole(rx.at[k, 2], dx.at[k, 2])

    for k in range(2):
        @pl.when(b == (r0, LAST)[k])
        def _():
            mine(k).wait()
    for m in own_h:
        m.wait()

    @pl.loop(1, 16)
    def _(i):
        rdma(hbuf.at[b], hbuf.at[b], hs.at[0], hr.at[0, i], partner).wait_send()
        rdma(piv, pbuf.at[b], hs.at[1], hr.at[1, i], partner).wait_send()


def comm(r0, cbuf, rbuf, loads, piv):
    anyspec = pl.BlockSpec(memory_space=pl.ANY)
    dma = pltpu.SemaphoreType.DMA
    return pl.pallas_call(
        functools.partial(comm_kernel, r0),
        out_shape=(
            jax.ShapeDtypeStruct(cbuf.shape, F32),
            jax.ShapeDtypeStruct(rbuf.shape, F32),
            jax.ShapeDtypeStruct((2, 2, 4, 64, W), F32),
            jax.ShapeDtypeStruct((16, 2, 1024), F32),
            jax.ShapeDtypeStruct((16, 2, 2 * W), F32),
        ),
        in_specs=[anyspec] * 4,
        out_specs=(anyspec,) * 5,
        input_output_aliases={0: 0, 1: 1},
        scratch_shapes=[
            dma((2, 4)), dma((2, 4)), dma((2, 4, N)),
            dma((2, 4)), dma((2, 3)), dma((2, 4, NR)), dma((2, 4)),
            dma((2, 4)), dma((2, 3)), dma((2, 4)), dma((2, 4)),
            dma((2,)), dma((2, 16)), dma((4,)),
        ],
        compiler_params=pltpu.CompilerParams(collective_id=r0, has_side_effects=True),
        name="exchange_%d" % r0,
    )(cbuf, rbuf, loads, piv)


def split(v):
    hi = v.astype(BF16)
    return hi, (v - hi.astype(F32)).astype(BF16)


def mm(a, b):
    return jnp.dot(a, b, preferred_element_type=F32)


def mm3(a, b):
    return mm(a[0], b[0]) + (mm(a[0], b[1]) + mm(a[1], b[0]))


def mm3t(a, b):
    dims = (((1,), (1,)), ((), ()))

    def one(p, q):
        return lax.dot_general(p, q, dims, preferred_element_type=F32)

    return one(a[0], b[0]) + (one(a[0], b[1]) + one(a[1], b[0]))


def full(a, b):
    return jnp.dot(a, b, precision=HIGH, preferred_element_type=F32)


def newton(pivot):
    n = pivot.shape[0]
    r = lax.broadcasted_iota(jnp.int32, (n, n), 0)
    c = lax.broadcasted_iota(jnp.int32, (n, n), 1)
    eye = r == c
    kept = jnp.where(eye, pivot, 0.0)
    drow = 1.0 / jnp.sum(kept, axis=0, keepdims=True)
    dcol = 1.0 / jnp.sum(kept, axis=1, keepdims=True)
    inv = jnp.where(eye, 2.0 * drow, 0.0) - dcol * (pivot * drow)
    for _ in range(NS_STEPS - 1):
        inv = 2.0 * inv - full(inv, full(pivot, inv))
    return inv


def update_kernel(weight, sc, fill, front, shift, cbuf, rbuf, dbuf, hbuf, pbuf, out, hout,
                  x0h, x0l, x1h, x1l, d1h, d1l, uh, ul, pvh, pvl, hs, weave):
    u = pl.program_id(0)
    s0, g, b = sc[0], lax.axis_index("grp"), lax.axis_index("blk")
    r0, q0 = s0 // 8, (s0 % 8) // 2
    cols = front.shape[1]
    ids = lax.broadcasted_iota(jnp.int32, (1, cols), 1) // W
    dead0 = (g == r0) & (ids == q0)
    dead1 = (g == LAST) & (ids == 3)

    @pl.when(u == 0)
    def _():
        d = [[dbuf[i, j].reshape(W, W) for j in range(2)] for i in range(2)]
        x0 = newton(d[0][0])
        m = full(d[1][0], x0)
        x1 = newton(d[1][1] - full(m, d[0][1]))
        x0h[...], x0l[...] = split(x0)
        x1h[...], x1l[...] = split(x1)
        d1h[...], d1l[...] = split(d[0][1])
        ms = split(m)
        u0 = jnp.where(dead0, 0.0, rbuf[0])
        u0s = split(u0)
        u1 = jnp.where(dead0 | dead1, 0.0, rbuf[1] - mm3(ms, u0s))
        u1s = split(u1)
        uh[0:W], ul[0:W] = u0s
        uh[W : 2 * W], ul[W : 2 * W] = u1s
        pv = jnp.concatenate([pbuf[:, 0, :], pbuf[:, 1, :]], axis=0)
        p0 = split(pv[:, 0:W])
        p1 = split(pv[:, W : 2 * W] - mm3t(p0, ms))
        pvh[:, 0:W], pvl[:, 0:W] = p0
        pvh[:, W : 2 * W], pvl[:, W : 2 * W] = p1

    aq = quarter_of(u, s0, b)
    gone0 = (b == r0) & (aq == q0)
    gone1 = (b == LAST) & (aq == 3)
    c0 = cbuf[0].reshape(W, W)
    l0 = mm3(split(c0), (x0h[...], x0l[...]))
    l0 = jnp.where(gone0, 0.0, l0)
    l0s = split(l0)
    c1 = cbuf[1].reshape(W, W) - mm3(l0s, (d1h[...], d1l[...]))
    l1 = mm3(split(c1), (x1h[...], x1l[...]))
    l1 = jnp.where(gone0 | gone1, 0.0, l1)
    l1s = split(l1)
    lh = jnp.concatenate([l0s[0], l1s[0]], axis=1)
    ll = jnp.concatenate([l0s[1], l1s[1]], axis=1)
    for j in range(cols // W):
        sl = slice(j * W, (j + 1) * W)
        f = masked(weight, front[:, sl], 2, 2, aq * 2, j * 2, fill, shift, g == b)
        f = f - mm3((lh, ll), (uh[:, sl], ul[:, sl]))
        f = jnp.where((g == r0) & (q0 == j) & jnp.logical_not(gone0), l0, f)
        if j == 3:
            f = jnp.where(g == LAST, jnp.where(gone0 | gone1, c1, l1), f)
        out[:, sl] = f
    here = pl.ds(pl.multiple_of(aq * W, W), W)
    h = jnp.concatenate([hbuf[:, 0, here], hbuf[:, 1, here]], axis=0)
    h = h - mm3t((pvh[...], pvl[...]), (lh, ll))
    hs[:, here] = h

    @pl.when(u == 3)
    def _():
        for j in range(cols // BS):
            lanes = slice(j * BS, (j + 1) * BS)
            weave[j, pl.ds(0, 16, stride=2), :] = hs[0:16, lanes]
            weave[j, pl.ds(1, 16, stride=2), :] = hs[16:32, lanes]
            hout[:, lanes] = weave[j]


def per_device(front, diag, fill, supernodes, loads):
    rows, cols = front.shape
    order = rows * lax.axis_size("blk")
    sc = supernodes
    weight = math.sqrt(order)
    shift = diag.reshape(rows // BS, BS)
    smem = pl.BlockSpec(memory_space=pltpu.SMEM)

    def const(shape):
        return pl.BlockSpec(shape, lambda u, sc: (0,) * len(shape))

    cbuf, rbuf, piv = pl.pallas_call(
        functools.partial(prep_kernel, weight),
        out_shape=(
            jax.ShapeDtypeStruct((2, 4, 256, W), F32),
            jax.ShapeDtypeStruct((2, W, cols), F32),
            jax.ShapeDtypeStruct((2, 2 * W), F32),
        ),
        grid_spec=pltpu.PrefetchScalarGridSpec(
            num_scalar_prefetch=1,
            grid=(4,),
            in_specs=[
                smem,
                pl.BlockSpec((W, cols), lambda u, sc: (quarter_of(u, sc[0], lax.axis_index("blk")), 0)),
                pl.BlockSpec((W, W), lambda u, sc: ((sc[0] % 8) // 2, u)),
                pl.BlockSpec((W, W), lambda u, sc: (3, u)),
                const(shift.shape),
                const(loads.shape),
            ],
            out_specs=(
                pl.BlockSpec((2, 4, 64, W), lambda u, sc: (0, 0, u, 0)),
                pl.BlockSpec((2, W, W), lambda u, sc: (0, 0, u)),
                const((2, 2 * W)),
            ),
        ),
        name="panels",
    )(sc, fill, front, front, front, shift, loads)
    rbuf = rbuf.reshape(2, 2, 4, 32, cols)
    cbuf, rbuf, dbuf, hbuf, pbuf = lax.switch(
        supernodes[0] // 8, [functools.partial(comm, r) for r in range(16)], cbuf, rbuf, loads, piv)
    rbuf = rbuf.reshape(2, W, cols)
    out, hout = pl.pallas_call(
        functools.partial(update_kernel, weight),
        out_shape=(
            jax.ShapeDtypeStruct((rows, cols), F32),
            jax.ShapeDtypeStruct((32, rows), F32),
        ),
        grid_spec=pltpu.PrefetchScalarGridSpec(
            num_scalar_prefetch=1,
            grid=(4,),
            in_specs=[
                smem,
                pl.BlockSpec((W, cols), lambda u, sc: (quarter_of(u, sc[0], lax.axis_index("blk")), 0)),
                const(shift.shape),
                pl.BlockSpec((2, 4, 64, W), lambda u, sc: (0, 0, u, 0)),
                const(rbuf.shape),
                const(dbuf.shape),
                const(hbuf.shape),
                const(pbuf.shape),
            ],
            out_specs=(
                pl.BlockSpec((W, cols), lambda u, sc: (quarter_of(u, sc[0], lax.axis_index("blk")), 0)),
                const((32, rows)),
            ),
            scratch_shapes=[pltpu.VMEM((W, W), BF16)] * 6
            + [pltpu.VMEM((2 * W, cols), BF16)] * 2
            + [pltpu.VMEM((32, 2 * W), BF16)] * 2
            + [pltpu.VMEM((32, rows), F32), pltpu.VMEM((rows // BS, 32, BS), F32)],
        ),
        name="update",
    )(sc, fill, front, shift, cbuf, rbuf, dbuf, hbuf, pbuf)
    return out, hout


def solution(mesh):
    in_specs = (P("blk", "grp"), P("blk"), P("blk", "grp"), P(), P(("grp", "blk"), None))
    out_specs = (P("blk", "grp"), P("grp", "blk"))
    return jax.shard_map(
        per_device, mesh=mesh, in_specs=in_specs, out_specs=out_specs, check_vma=False
    )
```

```python
import functools
import math

import jax
import jax.numpy as jnp
from jax import lax
from jax.experimental import pallas as pl
from jax.experimental.pallas import tpu as pltpu
from jax.sharding import PartitionSpec as P

MESH = pl.DeviceIdType.MESH
HIGH = lax.Precision.HIGHEST
F32 = jnp.float32
BF16 = jnp.bfloat16

BS = 128
W = 256
NS_STEPS = 3
CH = 32
N = 256 // CH
LG = 1
NR = 4
LAST = 15


def quarter_of(u, s0, b):
    r0, q0 = s0 // 8, (s0 % 8) // 2
    first = jnp.where(b == r0, q0, jnp.where(b == LAST, 3, 0))
    both = (b == r0) & (b == LAST)

    def swap(v):
        return jnp.where(v == 0, first, jnp.where(v == first, 0, v))

    v = jnp.where(both & (u == 1), 3, jnp.where(both & (u == 3), 1, u))
    return swap(v)


def masked(weight, values, rows, cols, row0, col0, fill_ref, shift, on_diag):
    out = []
    for i in range(rows):
        line = []
        for j in range(cols):
            v = values[i * BS : (i + 1) * BS, j * BS : (j + 1) * BS]
            v = jnp.where(fill_ref[row0 + i, col0 + j] > 0, v, 0.0)
            same = on_diag & (row0 + i == col0 + j)
            r = lax.broadcasted_iota(jnp.int32, (BS, BS), 0)
            c = lax.broadcasted_iota(jnp.int32, (BS, BS), 1)
            d = shift[pl.ds(row0 + i, 1), :] * weight
            v = v + jnp.where((r == c) & same, d, 0.0)
            line.append(v)
        out.append(jnp.concatenate(line, axis=1) if cols > 1 else line[0])
    return jnp.concatenate(out, axis=0) if rows > 1 else out[0]


def prep_kernel(weight, sc, fill, left0, left1, top0, top1, shift, loads, cbuf, rbuf, piv):
    u = pl.program_id(0)
    s0, g, b = sc[0], lax.axis_index("grp"), lax.axis_index("blk")
    q0 = (s0 % 8) // 2
    aq = quarter_of(u, s0, b)
    diag = g == b
    for k, q in ((0, q0), (1, 3)):
        v = (left0, left1)[k][...]
        v = masked(weight, v, 2, 2, aq * 2, q * 2, fill, shift, diag)
        cbuf[k] = v.reshape(4, 64, W)
        t = (top0, top1)[k][...]
        rbuf[k] = masked(weight, t, 2, 2, q * 2, u * 2, fill, shift, diag)
    piv[:, 0:W] = loads[:, pl.ds(pl.multiple_of(s0 * BS, W), W)]
    piv[:, W : 2 * W] = loads[:, loads.shape[1] - W :]


def comm_kernel(r0, cin, rin, loads, piv, cbuf, rbuf, dbuf, hbuf, pbuf,
                cs, cz, cr, rs, rx, rown, roth, ds, dx, down, doth, hs, hr, loc):
    g, b = lax.axis_index("grp"), lax.axis_index("blk")
    y, zl = g // 4, g % 4
    x, zh, c = b // 4, (b // 2) % 2, b % 2
    partner = {"blk": x * 4 + zh * 2 + (1 - c)}
    cross = {"blk": x * 4 + (1 - zh) * 2 + c}

    def xto(i):
        return {"blk": ((x + i) % 4) * 4 + zh * 2 + c}

    def yto(i):
        return {"grp": ((y + i) % 4) * 4 + zl}

    def zto(i):
        return {"grp": y * 4 + i}

    barrier = pltpu.get_barrier_semaphore()

    @pl.loop(1, 16)
    def _(i):
        pl.semaphore_signal(barrier, inc=1, device_id={"blk": (b + i) % 16}, device_id_type=MESH)

    @pl.loop(1, 4)
    def _(i):
        pl.semaphore_signal(barrier, inc=1, device_id=yto(i), device_id_type=MESH)
        pl.semaphore_signal(barrier, inc=1, device_id=zto((zl + i) % 4), device_id_type=MESH)

    pl.semaphore_wait(barrier, 21)

    def rdma(src, dst, ssem, rsem, to):
        return pltpu.make_async_remote_copy(
            src_ref=src, dst_ref=dst, send_sem=ssem, recv_sem=rsem, device_id=to, device_id_type=MESH)

    nots = jnp.logical_not
    place = (0, 1 if r0 == LAST else 0)

    def pick(k, first, second):
        return jnp.where(k == 0, first, second)

    def way(cls):
        return jnp.where(cls < 2, 1, 3), jnp.where(cls < 2, 3, 1)

    def ring(pos, root):
        a = (pos + 4 - root) % 4
        own = jnp.where(a == 3, 2, jnp.where(a == 2, 3, a))
        return a, own, jnp.where(a == 3, 1, a)

    def cplan(k):
        yk, zk = pick(k, r0 // 4, LAST // 4), pick(k, r0 % 4, LAST % 4)
        a, own, hop = ring(y, yk)
        e = jnp.where(zl > zk, zl - zk, zk - zl)
        lag = (jnp.where(a == 0, 0, 1) + jnp.where(e == 0, 0, jnp.where(e >= reach, 2, 1))) * LG
        return a, own, e == 0, lag, zk

    def rplan(k):
        xk, hk, ck = pick(k, r0 // 4, 3), pick(k, (r0 // 2) % 2, 1), pick(k, r0 % 2, 1)
        a, own, hop = ring(x, xk)
        inside = zh == hk
        lag = (hop + jnp.where(inside, 0, 2) + jnp.where(c == ck, 0, 1)) * LG
        return a, own, inside, lag, inside & (a == 0) & (c == ck), inside & (a == 0) & (c != ck)

    def waits(a, own, inside, origin, cls):
        return jnp.where(inside, nots(origin) & (a == way(cls)[1]), cls != own)

    reach = 4 if r0 % 4 < 2 else 3

    def relay(zk):
        return (((zk == 0) & (zl == 2)) | ((zk == 3) & (zl == 1))) & (reach == 3)

    def goes(a, cls):
        return (a != way(cls)[1]) & nots((cls == 3) & (a == 3))

    def cwaits(a, own, inside, cls):
        return jnp.where(inside, (a != 0) & nots(goes(a, cls)), cls != own)

    def crow(k, cls, n):
        return cbuf.at[k, cls, pl.ds(pl.multiple_of(n * CH, CH), CH), :]

    def csend(k, cls, n, sem, to):
        rdma(crow(k, cls, n), crow(k, cls, n), sem, cr.at[k, cls, n], to).start()

    def cwait(k, cls, n):
        rdma(crow(k, cls, n), crow(k, cls, n), cs.at[k, 0], cr.at[k, cls, n], yto(1)).wait_recv()

    def rrow(k, half, cls, n):
        return rbuf.at[k, half, cls, pl.ds(pl.multiple_of(n * 8, 8), 8), :]

    def rsend(k, half, cls, n, sem, to):
        rdma(rrow(k, half, cls, n), rrow(k, half, cls, n), sem, rown.at[k, cls, n], to).start()

    def rwait(k, cls, n):
        rdma(rrow(k, c, cls, n), rrow(k, c, cls, n), rs.at[k, 0], rown.at[k, cls, n], xto(1)).wait_recv()

    def drow(k, cls, half):
        return dbuf.at[k, :, cls, pl.ds(pl.multiple_of(half * 32, 32), 32), :]

    def dsource(k, cls, half):
        at = pl.multiple_of(pick(k, place[0], place[1]) * 64 + half * 32, 32)
        return cbuf.at[:, cls, pl.ds(at, 32), :]

    def dsend(k, cls, sem, to):
        rdma(drow(k, cls, c), drow(k, cls, c), sem, down.at[k, cls], to).start()

    def dwait(k, cls):
        rdma(drow(k, cls, c), drow(k, cls, c), ds.at[k, 0], down.at[k, cls], xto(1)).wait_recv()

    def passing(k, a, n, count):
        @pl.loop(0, count)
        def _(cls):
            @pl.when(goes(a, cls))
            def _():
                @pl.when(a != 0)
                def _():
                    cwait(k, cls, n)

                csend(k, cls, n, cs.at[k, cls], yto(way(cls)[0]))

    early = [(p + 1) * (64 // CH) for p in place]
    span = (3 if reach == 3 else 2) * LG
    tds = [span + e - 1 for e in early]
    turns = max(N + 3 * LG, max(tds) + 1 + 5 * LG)

    def cfinal(lo, hi):
        @pl.loop(0, 2)
        def _(k):
            a, own, inside, lag, zk = cplan(k)

            @pl.loop(0, 4)
            def _(cls):
                @pl.when(cwaits(a, own, inside, cls))
                def _():
                    @pl.loop(lo, hi)
                    def _(n):
                        cwait(k, cls, n)

    def mine(k):
        return pltpu.make_async_copy(cbuf.at[:, :, pl.ds(place[k] * 64, 64), :], dbuf.at[k], loc.at[2 + k])

    own_h = [
        pltpu.make_async_copy(loads.at[:, pl.ds(pl.multiple_of(b * 1024, 1024), 1024)], hbuf.at[b], loc.at[0]),
        pltpu.make_async_copy(piv, pbuf.at[b], loc.at[1]),
    ]

    @pl.loop(0, turns)
    def _(t):
        @pl.loop(0, 2)
        def _(k):
            a, own, inside, lag, zk = cplan(k)
            n = t - lag
            on = (n >= 0) & (n < N)

            @pl.when(on & inside)
            def _():
                @pl.when(a == 2)
                def _():
                    cwait(k, 3, n)
                    csend(k, 3, n, cs.at[k, 3], yto(3))

                @pl.when(a != 2)
                def _():
                    @pl.when(a == 0)
                    def _():
                        csend(k, 3, n, cz.at[k, zl], yto(2))

                    passing(k, a, n, 4)

                @pl.loop(0, 4)
                def _(z):
                    @pl.when((z != zl) & (z - zl < reach) & (zl - z < reach))
                    def _():
                        csend(k, own, n, cz.at[k, z], zto(z))

            late = n - LG

            @pl.when(inside & (a == 2) & (late >= 0) & (late < N))
            def _():
                passing(k, a, late, 3)

            @pl.when(on & nots(inside))
            def _():
                cwait(k, own, n)

                @pl.when(relay(zk))
                def _():
                    csend(k, own, n, cz.at[k, 0], zto(3 - zk))

                @pl.loop(1, 4)
                def _(i):
                    j = jnp.where(i == 1, 2, jnp.where(i == 2, 1, 3))
                    csend(k, own, n, cs.at[k, j], yto(j))

            a, own, inside, lag, root, mate = rplan(k)
            n = t - lag
            on = (n >= 0) & (n < NR)

            @pl.when(on & inside)
            def _():
                @pl.loop(0, 4)
                def _(cls):
                    step, end = way(cls)

                    @pl.when(root)
                    def _():
                        rsend(k, 1 - c, cls, n, rx.at[k, 1], partner)

                    @pl.when(a != end)
                    def _():
                        @pl.when(nots(root))
                        def _():
                            rwait(k, cls, n)

                        rsend(k, c, cls, n, rs.at[k, cls], xto(step))

                rsend(k, c, own, n, rx.at[k, 0], cross)

            @pl.when(on & nots(inside))
            def _():
                rwait(k, own, n)

                @pl.loop(1, 4)
                def _(i):
                    j = jnp.where(i == 1, 2, jnp.where(i == 2, 1, 3))
                    rsend(k, c, own, n, rs.at[k, j], xto(j))

        @pl.when(t == 2)
        def _():
            for m in own_h:
                m.start()

            @pl.loop(1, 16)
            def _(i):
                to = (b + i) % 16
                cols = pl.ds(pl.multiple_of(to * 1024, 1024), 1024)
                rdma(loads.at[:, cols], hbuf.at[b], hs.at[0], hr.at[0, i], {"blk": to}).start()
                rdma(piv, pbuf.at[b], hs.at[1], hr.at[1, i], {"blk": to}).start()

        for i, td in enumerate(sorted(set(tds))):
            @pl.when(t == td)
            def _():
                cfinal(0 if i == 0 else early[0], td - span + 1)
                for k in range(2):
                    if tds[k] == td:
                        @pl.when(b == (r0, LAST)[k])
                        def _():
                            mine(k).start()

        @pl.loop(0, 2)
        def _(k):
            a, own, inside, lag, root, mate = rplan(k)
            on = t - lag == pick(k, tds[0], tds[1])

            @pl.when(on & inside)
            def _():
                @pl.loop(0, 4)
                def _(cls):
                    step, end = way(cls)

                    @pl.when(root)
                    def _():
                        rdma(dsource(k, cls, 1 - c), drow(k, cls, 1 - c), dx.at[k, 1], down.at[k, cls],
                             partner).start()
                        rdma(dsource(k, cls, c), drow(k, cls, c), ds.at[k, cls], down.at[k, cls],
                             xto(step)).start()

                    @pl.when(nots(root) & (a != end))
                    def _():
                        dwait(k, cls)
                        dsend(k, cls, ds.at[k, cls], xto(step))

                @pl.when(root)
                def _():
                    rdma(dsource(k, 0, c), drow(k, 0, c), dx.at[k, 0], down.at[k, 0], cross).start()

                    @pl.loop(0, 4)
                    def _(cls):
                        rdma(dsource(k, cls, c), drow(k, cls, c), dx.at[k, 2], doth.at[k, cls], partner).start()

                @pl.when(nots(root))
                def _():
                    dsend(k, own, dx.at[k, 0], cross)

            @pl.when(on & nots(inside))
            def _():
                dwait(k, own)

                @pl.loop(1, 4)
                def _(i):
                    j = jnp.where(i == 1, 2, jnp.where(i == 2, 1, 3))
                    dsend(k, own, ds.at[k, j], xto(j))

    @pl.loop(0, 2)
    def _(k):
        a, own, inside, lag, root, mate = rplan(k)

        @pl.loop(0, 4)
        def _(cls):
            @pl.when(waits(a, own, inside, a == 0, cls))
            def _():
                @pl.loop(0, NR)
                def _(n):
                    rwait(k, cls, n)

            @pl.when(nots(mate))
            def _():
                half = rbuf.at[k, c, cls]
                rdma(half, half, rx.at[k, 2], roth.at[k, cls], partner).start()

    @pl.loop(0, 2)
    def _(k):
        a, own, inside, lag, root, mate = rplan(k)

        @pl.loop(0, 4)
        def _(cls):
            @pl.when(waits(a, own, inside, a == 0, cls))
            def _():
                dwait(k, cls)

            @pl.when(nots(mate | root))
            def _():
                rdma(drow(k, cls, c), drow(k, cls, c), dx.at[k, 2], doth.at[k, cls], partner).start()

    cfinal(max(early), N)

    @pl.loop(1, 16)
    def _(i):
        rdma(piv, pbuf.at[b], hs.at[1], hr.at[1, i], partner).wait_recv()
        rdma(hbuf.at[b], hbuf.at[b], hs.at[0], hr.at[0, i], partner).wait_recv()

    @pl.loop(0, 2)
    def _(k):
        a, own, inside, lag, root, mate = rplan(k)

        @pl.when(nots(root))
        def _():
            @pl.loop(0, 4)
            def _(cls):
                rest = rbuf.at[k, 1 - c, cls]
                rdma(rest, rest, rx.at[k, 2], roth.at[k, cls], partner).wait_recv()
                part = drow(k, cls, 1 - c)
                rdma(part, part, dx.at[k, 2], doth.at[k, cls], partner).wait_recv()

    @pl.loop(0, 2)
    def _(k):
        ca, cown, cin_, clag, zk = cplan(k)
        a, own, inside, lag, root, mate = rplan(k)

        def csent(sem):
            rdma(cbuf.at[k, 0], cbuf.at[k, 0], sem, cr.at[k, 0, 0], yto(1)).wait_send()

        def rsent(sem):
            rdma(rbuf.at[k, c, 0], rbuf.at[k, c, 0], sem, rown.at[k, 0, 0], xto(1)).wait_send()

        def dsent(sem):
            rdma(drow(k, 0, c), drow(k, 0, c), sem, down.at[k, 0], xto(1)).wait_send()

        @pl.loop(0, 4)
        def _(i):
            @pl.when(jnp.where(cin_, goes(ca, i), i > 0))
            def _():
                csent(cs.at[k, i])

            @pl.when(jnp.where(inside, a != way(i)[1], i > 0))
            def _():
                rsent(rs.at[k, i])
                dsent(ds.at[k, i])

            near = jnp.where(i == zl, ca == 0, (i - zl < reach) & (zl - i < reach))

            @pl.when(jnp.where(cin_, near, (i == 0) & relay(zk)))
            def _():
                csent(cz.at[k, i])

        @pl.when(inside)
        def _():
            rsent(rx.at[k, 0])
            dsent(dx.at[k, 0])

        def whole(sem, dsem):
            rdma(rbuf.at[k, 0], rbuf.at[k, 0], sem, rown.at[k, 0, 0], xto(1)).wait_send()
            part = dbuf.at[k, :, :, 0:32, :]
            rdma(part, part, dsem, down.at[k, 0], xto(1)).wait_send()

        @pl.when(root)
        def _():
            whole(rx.at[k, 1], dx.at[k, 1])

        @pl.when(nots(mate))
        def _():
            whole(rx.at[k, 2], dx.at[k, 2])

    for k in range(2):
        @pl.when(b == (r0, LAST)[k])
        def _():
            mine(k).wait()
    for m in own_h:
        m.wait()

    @pl.loop(1, 16)
    def _(i):
        rdma(hbuf.at[b], hbuf.at[b], hs.at[0], hr.at[0, i], partner).wait_send()
        rdma(piv, pbuf.at[b], hs.at[1], hr.at[1, i], partner).wait_send()


def comm(r0, cbuf, rbuf, loads, piv):
    anyspec = pl.BlockSpec(memory_space=pl.ANY)
    dma = pltpu.SemaphoreType.DMA
    return pl.pallas_call(
        functools.partial(comm_kernel, r0),
        out_shape=(
            jax.ShapeDtypeStruct(cbuf.shape, F32),
            jax.ShapeDtypeStruct(rbuf.shape, F32),
            jax.ShapeDtypeStruct((2, 2, 4, 64, W), F32),
            jax.ShapeDtypeStruct((16, 2, 1024), F32),
            jax.ShapeDtypeStruct((16, 2, 2 * W), F32),
        ),
        in_specs=[anyspec] * 4,
        out_specs=(anyspec,) * 5,
        input_output_aliases={0: 0, 1: 1},
        scratch_shapes=[
            dma((2, 4)), dma((2, 4)), dma((2, 4, N)),
            dma((2, 4)), dma((2, 3)), dma((2, 4, NR)), dma((2, 4)),
            dma((2, 4)), dma((2, 3)), dma((2, 4)), dma((2, 4)),
            dma((2,)), dma((2, 16)), dma((4,)),
        ],
        compiler_params=pltpu.CompilerParams(collective_id=r0, has_side_effects=True),
        name="exchange_%d" % r0,
    )(cbuf, rbuf, loads, piv)


def split(v):
    hi = v.astype(BF16)
    return hi, (v - hi.astype(F32)).astype(BF16)


def mm(a, b):
    return jnp.dot(a, b, preferred_element_type=F32)


def mm3(a, b):
    return mm(a[0], b[0]) + (mm(a[0], b[1]) + mm(a[1], b[0]))


def mm3t(a, b):
    dims = (((1,), (1,)), ((), ()))

    def one(p, q):
        return lax.dot_general(p, q, dims, preferred_element_type=F32)

    return one(a[0], b[0]) + (one(a[0], b[1]) + one(a[1], b[0]))


def full(a, b):
    return mm3(split(a), split(b))


def newton(pivot):
    n = pivot.shape[0]
    r = lax.broadcasted_iota(jnp.int32, (n, n), 0)
    c = lax.broadcasted_iota(jnp.int32, (n, n), 1)
    eye = r == c
    kept = jnp.where(eye, pivot, 0.0)
    drow = 1.0 / jnp.sum(kept, axis=0, keepdims=True)
    dcol = 1.0 / jnp.sum(kept, axis=1, keepdims=True)
    inv = jnp.where(eye, 2.0 * drow, 0.0) - dcol * (pivot * drow)
    for _ in range(NS_STEPS - 1):
        inv = 2.0 * inv - full(inv, full(pivot, inv))
    return inv


def update_kernel(weight, sc, fill, front, shift, cbuf, rbuf, dbuf, hbuf, pbuf, out, hout,
                  x0h, x0l, t1h, t1l, later, uh, ul, pvh, pvl, hs, weave):
    u = pl.program_id(0)
    s0, g, b = sc[0], lax.axis_index("grp"), lax.axis_index("blk")
    r0, q0 = s0 // 8, (s0 % 8) // 2
    cols = front.shape[1]
    ids = lax.broadcasted_iota(jnp.int32, (1, cols), 1) // W
    dead0 = (g == r0) & (ids == q0)
    dead1 = (g == LAST) & (ids == 3)

    @pl.when(u == 0)
    def _():
        d = [[dbuf[i, j].reshape(W, W) for j in range(2)] for i in range(2)]
        x0 = newton(d[0][0])
        m = full(d[1][0], x0)
        d11 = d[1][1] - full(m, d[0][1])
        x1 = newton(d11)
        x0h[...], x0l[...] = split(x0)
        t1h[0:W], t1l[0:W] = split(-full(full(x0, d[0][1]), x1))
        t1h[W : 2 * W], t1l[W : 2 * W] = split(x1)
        later[...] = d11
        ms = split(m)
        u0 = jnp.where(dead0, 0.0, rbuf[0])
        u0s = split(u0)
        u1 = jnp.where(dead0 | dead1, 0.0, rbuf[1] - mm3(ms, u0s))
        u1s = split(u1)
        uh[0:W], ul[0:W] = u0s
        uh[W : 2 * W], ul[W : 2 * W] = u1s
        pv = jnp.concatenate([pbuf[:, 0, :], pbuf[:, 1, :]], axis=0)
        p0 = split(pv[:, 0:W])
        p1 = split(pv[:, W : 2 * W] - mm3t(p0, ms))
        pvh[:, 0:W], pvl[:, 0:W] = p0
        pvh[:, W : 2 * W], pvl[:, W : 2 * W] = p1

    aq = quarter_of(u, s0, b)
    gone0 = (b == r0) & (aq == q0)
    gone1 = (b == LAST) & (aq == 3)
    c1 = cbuf[1].reshape(W, W)
    c0s, c1s = split(cbuf[0].reshape(W, W)), split(c1)
    both = tuple(jnp.concatenate([p, q], axis=1) for p, q in zip(c0s, c1s))
    l0 = jnp.where(gone0, 0.0, mm3(c0s, (x0h[...], x0l[...])))
    l1 = jnp.where(gone0 | gone1, 0.0, mm3(both, (t1h[...], t1l[...])))
    l0s, l1s = split(l0), split(l1)
    lh = jnp.concatenate([l0s[0], l1s[0]], axis=1)
    ll = jnp.concatenate([l0s[1], l1s[1]], axis=1)
    for j in range(cols // W):
        sl = slice(j * W, (j + 1) * W)
        f = masked(weight, front[:, sl], 2, 2, aq * 2, j * 2, fill, shift, g == b)
        f = f - mm3((lh, ll), (uh[:, sl], ul[:, sl]))
        f = jnp.where((g == r0) & (q0 == j) & jnp.logical_not(gone0), l0, f)
        if j == 3:
            f = jnp.where(g == LAST, jnp.where(gone0, c1, jnp.where(gone1, later[...], l1)), f)
        out[:, sl] = f
    here = pl.ds(pl.multiple_of(aq * W, W), W)
    h = jnp.concatenate([hbuf[:, 0, here], hbuf[:, 1, here]], axis=0)
    h = h - mm3t((pvh[...], pvl[...]), (lh, ll))
    hs[:, here] = h

    @pl.when(u == 3)
    def _():
        for j in range(cols // BS):
            lanes = slice(j * BS, (j + 1) * BS)
            weave[j, pl.ds(0, 16, stride=2), :] = hs[0:16, lanes]
            weave[j, pl.ds(1, 16, stride=2), :] = hs[16:32, lanes]
            hout[:, lanes] = weave[j]


def per_device(front, diag, fill, supernodes, loads):
    rows, cols = front.shape
    order = rows * lax.axis_size("blk")
    sc = supernodes
    weight = math.sqrt(order)
    shift = diag.reshape(rows // BS, BS)
    smem = pl.BlockSpec(memory_space=pltpu.SMEM)

    def const(shape):
        return pl.BlockSpec(shape, lambda u, sc: (0,) * len(shape))

    cbuf, rbuf, piv = pl.pallas_call(
        functools.partial(prep_kernel, weight),
        out_shape=(
            jax.ShapeDtypeStruct((2, 4, 256, W), F32),
            jax.ShapeDtypeStruct((2, W, cols), F32),
            jax.ShapeDtypeStruct((2, 2 * W), F32),
        ),
        grid_spec=pltpu.PrefetchScalarGridSpec(
            num_scalar_prefetch=1,
            grid=(4,),
            in_specs=[
                smem,
                pl.BlockSpec((W, W), lambda u, sc: (quarter_of(u, sc[0], lax.axis_index("blk")), (sc[0] % 8) // 2)),
                pl.BlockSpec((W, W), lambda u, sc: (quarter_of(u, sc[0], lax.axis_index("blk")), 3)),
                pl.BlockSpec((W, W), lambda u, sc: ((sc[0] % 8) // 2, u)),
                pl.BlockSpec((W, W), lambda u, sc: (3, u)),
                const(shift.shape),
                const(loads.shape),
            ],
            out_specs=(
                pl.BlockSpec((2, 4, 64, W), lambda u, sc: (0, 0, u, 0)),
                pl.BlockSpec((2, W, W), lambda u, sc: (0, 0, u)),
                const((2, 2 * W)),
            ),
        ),
        name="panels",
    )(sc, fill, front, front, front, front, shift, loads)
    rbuf = rbuf.reshape(2, 2, 4, 32, cols)
    cbuf, rbuf, dbuf, hbuf, pbuf = lax.switch(
        supernodes[0] // 8, [functools.partial(comm, r) for r in range(16)], cbuf, rbuf, loads, piv)
    rbuf = rbuf.reshape(2, W, cols)
    out, hout = pl.pallas_call(
        functools.partial(update_kernel, weight),
        out_shape=(
            jax.ShapeDtypeStruct((rows, cols), F32),
            jax.ShapeDtypeStruct((32, rows), F32),
        ),
        grid_spec=pltpu.PrefetchScalarGridSpec(
            num_scalar_prefetch=1,
            grid=(4,),
            in_specs=[
                smem,
                pl.BlockSpec((W, cols), lambda u, sc: (quarter_of(u, sc[0], lax.axis_index("blk")), 0)),
                const(shift.shape),
                pl.BlockSpec((2, 4, 64, W), lambda u, sc: (0, 0, u, 0)),
                const(rbuf.shape),
                const(dbuf.shape),
                const(hbuf.shape),
                const(pbuf.shape),
            ],
            out_specs=(
                pl.BlockSpec((W, cols), lambda u, sc: (quarter_of(u, sc[0], lax.axis_index("blk")), 0)),
                const((32, rows)),
            ),
            scratch_shapes=[pltpu.VMEM((W, W), BF16)] * 2
            + [pltpu.VMEM((2 * W, W), BF16)] * 2
            + [pltpu.VMEM((W, W), F32)]
            + [pltpu.VMEM((2 * W, cols), BF16)] * 2
            + [pltpu.VMEM((32, 2 * W), BF16)] * 2
            + [pltpu.VMEM((32, rows), F32), pltpu.VMEM((rows // BS, 32, BS), F32)],
        ),
        name="update",
    )(sc, fill, front, shift, cbuf, rbuf, dbuf, hbuf, pbuf)
    return out, hout


def solution(mesh):
    in_specs = (P("blk", "grp"), P("blk"), P("blk", "grp"), P(), P(("grp", "blk"), None))
    out_specs = (P("blk", "grp"), P("grp", "blk"))
    return jax.shard_map(
        per_device, mesh=mesh, in_specs=in_specs, out_specs=out_specs, check_vma=False
    )
```

```python
import functools
import math

import jax
import jax.numpy as jnp
from jax import lax
from jax.experimental import pallas as pl
from jax.experimental.pallas import tpu as pltpu
from jax.sharding import PartitionSpec as P

MESH = pl.DeviceIdType.MESH
HIGH = lax.Precision.HIGHEST
F32 = jnp.float32
BF16 = jnp.bfloat16

BS = 128
W = 256
NS_STEPS = 3
CH = 32
N = 256 // CH
LG = 1
NR = 4
LAST = 15


def quarter_of(u, s0, b):
    r0, q0 = s0 // 8, (s0 % 8) // 2
    first = jnp.where(b == r0, q0, jnp.where(b == LAST, 3, 0))
    both = (b == r0) & (b == LAST)

    def swap(v):
        return jnp.where(v == 0, first, jnp.where(v == first, 0, v))

    v = jnp.where(both & (u == 1), 3, jnp.where(both & (u == 3), 1, u))
    return swap(v)


def masked(weight, values, rows, cols, row0, col0, fill_ref, shift, on_diag):
    out = []
    for i in range(rows):
        line = []
        for j in range(cols):
            v = values[i * BS : (i + 1) * BS, j * BS : (j + 1) * BS]
            v = jnp.where(fill_ref[row0 + i, col0 + j] > 0, v, 0.0)
            same = on_diag & (row0 + i == col0 + j)
            r = lax.broadcasted_iota(jnp.int32, (BS, BS), 0)
            c = lax.broadcasted_iota(jnp.int32, (BS, BS), 1)
            d = shift[pl.ds(row0 + i, 1), :] * weight
            v = v + jnp.where((r == c) & same, d, 0.0)
            line.append(v)
        out.append(jnp.concatenate(line, axis=1) if cols > 1 else line[0])
    return jnp.concatenate(out, axis=0) if rows > 1 else out[0]


def prep_kernel(weight, sc, fill, left0, left1, top0, top1, shift, loads, cbuf, rbuf, piv):
    u = pl.program_id(0)
    s0, g, b = sc[0], lax.axis_index("grp"), lax.axis_index("blk")
    q0 = (s0 % 8) // 2
    aq = quarter_of(u, s0, b)
    diag = g == b
    for k, q in ((0, q0), (1, 3)):
        v = (left0, left1)[k][...]
        v = masked(weight, v, 2, 2, aq * 2, q * 2, fill, shift, diag)
        cbuf[k] = v.reshape(4, 64, W)
        t = (top0, top1)[k][...]
        rbuf[k] = masked(weight, t, 2, 2, q * 2, u * 2, fill, shift, diag)
    piv[:, 0:W] = loads[:, pl.ds(pl.multiple_of(s0 * BS, W), W)]
    piv[:, W : 2 * W] = loads[:, loads.shape[1] - W :]


def comm_kernel(r0, cin, rin, loads, piv, cbuf, rbuf, dbuf, hbuf, pbuf,
                cs, cz, cr, rs, rx, rown, roth, ds, dx, down, doth, hs, hr, loc):
    g, b = lax.axis_index("grp"), lax.axis_index("blk")
    y, zl = g // 4, g % 4
    x, zh, c = b // 4, (b // 2) % 2, b % 2
    partner = {"blk": x * 4 + zh * 2 + (1 - c)}
    cross = {"blk": x * 4 + (1 - zh) * 2 + c}

    def xto(i):
        return {"blk": ((x + i) % 4) * 4 + zh * 2 + c}

    def yto(i):
        return {"grp": ((y + i) % 4) * 4 + zl}

    def zto(i):
        return {"grp": y * 4 + i}

    barrier = pltpu.get_barrier_semaphore()

    @pl.loop(1, 16)
    def _(i):
        pl.semaphore_signal(barrier, inc=1, device_id={"blk": (b + i) % 16}, device_id_type=MESH)

    @pl.loop(1, 4)
    def _(i):
        pl.semaphore_signal(barrier, inc=1, device_id=yto(i), device_id_type=MESH)
        pl.semaphore_signal(barrier, inc=1, device_id=zto((zl + i) % 4), device_id_type=MESH)

    pl.semaphore_wait(barrier, 21)

    def rdma(src, dst, ssem, rsem, to):
        return pltpu.make_async_remote_copy(
            src_ref=src, dst_ref=dst, send_sem=ssem, recv_sem=rsem, device_id=to, device_id_type=MESH)

    nots = jnp.logical_not
    place = (0, 1 if r0 == LAST else 0)

    def pick(k, first, second):
        return jnp.where(k == 0, first, second)

    def way(cls):
        return jnp.where(cls < 2, 1, 3), jnp.where(cls < 2, 3, 1)

    def ring(pos, root):
        a = (pos + 4 - root) % 4
        own = jnp.where(a == 3, 2, jnp.where(a == 2, 3, a))
        return a, own, jnp.where(a == 3, 1, a)

    def cplan(k):
        yk, zk = pick(k, r0 // 4, LAST // 4), pick(k, r0 % 4, LAST % 4)
        a, own, hop = ring(y, yk)
        e = jnp.where(zl > zk, zl - zk, zk - zl)
        lag = (jnp.where(a == 0, 0, 1) + jnp.where(e == 0, 0, jnp.where(e >= reach, 2, 1))) * LG
        return a, own, e == 0, lag, zk

    def rplan(k):
        xk, hk, ck = pick(k, r0 // 4, 3), pick(k, (r0 // 2) % 2, 1), pick(k, r0 % 2, 1)
        a, own, hop = ring(x, xk)
        inside = zh == hk
        lag = (hop + jnp.where(inside, 0, 2) + jnp.where(c == ck, 0, 1)) * LG
        return a, own, inside, lag, inside & (a == 0) & (c == ck), inside & (a == 0) & (c != ck)

    def waits(a, own, inside, origin, cls):
        return jnp.where(inside, nots(origin) & (a == way(cls)[1]), cls != own)

    reach = 4 if r0 % 4 < 2 else 3

    def relay(zk):
        return (((zk == 0) & (zl == 2)) | ((zk == 3) & (zl == 1))) & (reach == 3)

    def goes(a, cls):
        return (a != way(cls)[1]) & nots((cls == 3) & (a == 3))

    def cwaits(a, own, inside, cls):
        return jnp.where(inside, (a != 0) & nots(goes(a, cls)), cls != own)

    def crow(k, cls, n):
        return cbuf.at[k, cls, pl.ds(pl.multiple_of(n * CH, CH), CH), :]

    def csend(k, cls, n, sem, to):
        rdma(crow(k, cls, n), crow(k, cls, n), sem, cr.at[k, cls, n], to).start()

    def cwait(k, cls, n):
        rdma(crow(k, cls, n), crow(k, cls, n), cs.at[k, 0], cr.at[k, cls, n], yto(1)).wait_recv()

    def rrow(k, half, cls, n):
        return rbuf.at[k, half, cls, pl.ds(pl.multiple_of(n * 8, 8), 8), :]

    def rsend(k, half, cls, n, sem, to):
        rdma(rrow(k, half, cls, n), rrow(k, half, cls, n), sem, rown.at[k, cls, n], to).start()

    def rwait(k, cls, n):
        rdma(rrow(k, c, cls, n), rrow(k, c, cls, n), rs.at[k, 0], rown.at[k, cls, n], xto(1)).wait_recv()

    def drow(k, cls, half):
        return dbuf.at[k, :, cls, pl.ds(pl.multiple_of(half * 32, 32), 32), :]

    def dsource(k, cls, half):
        at = pl.multiple_of(pick(k, place[0], place[1]) * 64 + half * 32, 32)
        return cbuf.at[:, cls, pl.ds(at, 32), :]

    def dsend(k, cls, sem, to):
        rdma(drow(k, cls, c), drow(k, cls, c), sem, down.at[k, cls], to).start()

    def dwait(k, cls):
        rdma(drow(k, cls, c), drow(k, cls, c), ds.at[k, 0], down.at[k, cls], xto(1)).wait_recv()

    def passing(k, a, n, count):
        @pl.loop(0, count)
        def _(cls):
            @pl.when(goes(a, cls))
            def _():
                @pl.when(a != 0)
                def _():
                    cwait(k, cls, n)

                csend(k, cls, n, cs.at[k, cls], yto(way(cls)[0]))

    early = [(p + 1) * (64 // CH) for p in place]
    span = (3 if reach == 3 else 2) * LG
    tds = [span + e - 1 for e in early]
    turns = max(N + 3 * LG, max(tds) + 1 + 5 * LG)

    def cfinal(lo, hi):
        @pl.loop(0, 2)
        def _(k):
            a, own, inside, lag, zk = cplan(k)

            @pl.loop(0, 4)
            def _(cls):
                @pl.when(cwaits(a, own, inside, cls))
                def _():
                    @pl.loop(lo, hi)
                    def _(n):
                        cwait(k, cls, n)

    def mine(k):
        return pltpu.make_async_copy(cbuf.at[:, :, pl.ds(place[k] * 64, 64), :], dbuf.at[k], loc.at[2 + k])

    own_h = [
        pltpu.make_async_copy(loads.at[:, pl.ds(pl.multiple_of(b * 1024, 1024), 1024)], hbuf.at[b], loc.at[0]),
        pltpu.make_async_copy(piv, pbuf.at[b], loc.at[1]),
    ]

    @pl.loop(0, turns)
    def _(t):
        @pl.loop(0, 2)
        def _(k):
            a, own, inside, lag, zk = cplan(k)
            n = t - lag
            on = (n >= 0) & (n < N)

            @pl.when(on & inside)
            def _():
                @pl.when(a == 2)
                def _():
                    cwait(k, 3, n)
                    csend(k, 3, n, cs.at[k, 3], yto(3))

                @pl.when(a != 2)
                def _():
                    @pl.when(a == 0)
                    def _():
                        csend(k, 3, n, cz.at[k, zl], yto(2))

                    passing(k, a, n, 4)

                @pl.loop(0, 4)
                def _(z):
                    @pl.when((z != zl) & (z - zl < reach) & (zl - z < reach))
                    def _():
                        csend(k, own, n, cz.at[k, z], zto(z))

            late = n - LG

            @pl.when(inside & (a == 2) & (late >= 0) & (late < N))
            def _():
                passing(k, a, late, 3)

            @pl.when(on & nots(inside))
            def _():
                cwait(k, own, n)

                @pl.when(relay(zk))
                def _():
                    csend(k, own, n, cz.at[k, 0], zto(3 - zk))

                @pl.loop(1, 4)
                def _(i):
                    j = jnp.where(i == 1, 2, jnp.where(i == 2, 1, 3))
                    csend(k, own, n, cs.at[k, j], yto(j))

            a, own, inside, lag, root, mate = rplan(k)
            n = t - lag
            on = (n >= 0) & (n < NR)

            @pl.when(on & inside)
            def _():
                @pl.loop(0, 4)
                def _(cls):
                    step, end = way(cls)

                    @pl.when(root)
                    def _():
                        rsend(k, 1 - c, cls, n, rx.at[k, 1], partner)

                    @pl.when(a != end)
                    def _():
                        @pl.when(nots(root))
                        def _():
                            rwait(k, cls, n)

                        rsend(k, c, cls, n, rs.at[k, cls], xto(step))

                rsend(k, c, own, n, rx.at[k, 0], cross)

            @pl.when(on & nots(inside))
            def _():
                rwait(k, own, n)

                @pl.loop(1, 4)
                def _(i):
                    j = jnp.where(i == 1, 2, jnp.where(i == 2, 1, 3))
                    rsend(k, c, own, n, rs.at[k, j], xto(j))

        @pl.when(t == 6)
        def _():
            for m in own_h:
                m.start()

            @pl.loop(1, 16)
            def _(i):
                to = (b + i) % 16
                cols = pl.ds(pl.multiple_of(to * 1024, 1024), 1024)
                rdma(loads.at[:, cols], hbuf.at[b], hs.at[0], hr.at[0, i], {"blk": to}).start()
                rdma(piv, pbuf.at[b], hs.at[1], hr.at[1, i], {"blk": to}).start()

        for i, td in enumerate(sorted(set(tds))):
            @pl.when(t == td)
            def _():
                cfinal(0 if i == 0 else early[0], td - span + 1)
                for k in range(2):
                    if tds[k] == td:
                        @pl.when(b == (r0, LAST)[k])
                        def _():
                            mine(k).start()

        @pl.loop(0, 2)
        def _(k):
            a, own, inside, lag, root, mate = rplan(k)
            on = t - lag == pick(k, tds[0], tds[1])

            @pl.when(on & inside)
            def _():
                @pl.loop(0, 4)
                def _(cls):
                    step, end = way(cls)

                    @pl.when(root)
                    def _():
                        rdma(dsource(k, cls, 1 - c), drow(k, cls, 1 - c), dx.at[k, 1], down.at[k, cls],
                             partner).start()
                        rdma(dsource(k, cls, c), drow(k, cls, c), ds.at[k, cls], down.at[k, cls],
                             xto(step)).start()

                    @pl.when(nots(root) & (a != end))
                    def _():
                        dwait(k, cls)
                        dsend(k, cls, ds.at[k, cls], xto(step))

                @pl.when(root)
                def _():
                    rdma(dsource(k, 0, c), drow(k, 0, c), dx.at[k, 0], down.at[k, 0], cross).start()

                    @pl.loop(0, 4)
                    def _(cls):
                        rdma(dsource(k, cls, c), drow(k, cls, c), dx.at[k, 2], doth.at[k, cls], partner).start()

                @pl.when(nots(root))
                def _():
                    dsend(k, own, dx.at[k, 0], cross)

            @pl.when(on & nots(inside))
            def _():
                dwait(k, own)

                @pl.loop(1, 4)
                def _(i):
                    j = jnp.where(i == 1, 2, jnp.where(i == 2, 1, 3))
                    dsend(k, own, ds.at[k, j], xto(j))

    @pl.loop(0, 2)
    def _(k):
        a, own, inside, lag, root, mate = rplan(k)

        @pl.loop(0, 4)
        def _(cls):
            @pl.when(waits(a, own, inside, a == 0, cls))
            def _():
                @pl.loop(0, NR)
                def _(n):
                    rwait(k, cls, n)

            @pl.when(nots(mate))
            def _():
                half = rbuf.at[k, c, cls]
                rdma(half, half, rx.at[k, 2], roth.at[k, cls], partner).start()

    @pl.loop(0, 2)
    def _(k):
        a, own, inside, lag, root, mate = rplan(k)

        @pl.loop(0, 4)
        def _(cls):
            @pl.when(waits(a, own, inside, a == 0, cls))
            def _():
                dwait(k, cls)

            @pl.when(nots(mate | root))
            def _():
                rdma(drow(k, cls, c), drow(k, cls, c), dx.at[k, 2], doth.at[k, cls], partner).start()

    cfinal(max(early), N)

    @pl.loop(1, 16)
    def _(i):
        rdma(piv, pbuf.at[b], hs.at[1], hr.at[1, i], partner).wait_recv()
        rdma(hbuf.at[b], hbuf.at[b], hs.at[0], hr.at[0, i], partner).wait_recv()

    @pl.loop(0, 2)
    def _(k):
        a, own, inside, lag, root, mate = rplan(k)

        @pl.when(nots(root))
        def _():
            @pl.loop(0, 4)
            def _(cls):
                rest = rbuf.at[k, 1 - c, cls]
                rdma(rest, rest, rx.at[k, 2], roth.at[k, cls], partner).wait_recv()
                part = drow(k, cls, 1 - c)
                rdma(part, part, dx.at[k, 2], doth.at[k, cls], partner).wait_recv()

    @pl.loop(0, 2)
    def _(k):
        ca, cown, cin_, clag, zk = cplan(k)
        a, own, inside, lag, root, mate = rplan(k)

        def csent(sem):
            rdma(cbuf.at[k, 0], cbuf.at[k, 0], sem, cr.at[k, 0, 0], yto(1)).wait_send()

        def rsent(sem):
            rdma(rbuf.at[k, c, 0], rbuf.at[k, c, 0], sem, rown.at[k, 0, 0], xto(1)).wait_send()

        def dsent(sem):
            rdma(drow(k, 0, c), drow(k, 0, c), sem, down.at[k, 0], xto(1)).wait_send()

        @pl.loop(0, 4)
        def _(i):
            @pl.when(jnp.where(cin_, goes(ca, i), i > 0))
            def _():
                csent(cs.at[k, i])

            @pl.when(jnp.where(inside, a != way(i)[1], i > 0))
            def _():
                rsent(rs.at[k, i])
                dsent(ds.at[k, i])

            near = jnp.where(i == zl, ca == 0, (i - zl < reach) & (zl - i < reach))

            @pl.when(jnp.where(cin_, near, (i == 0) & relay(zk)))
            def _():
                csent(cz.at[k, i])

        @pl.when(inside)
        def _():
            rsent(rx.at[k, 0])
            dsent(dx.at[k, 0])

        def whole(sem, dsem):
            rdma(rbuf.at[k, 0], rbuf.at[k, 0], sem, rown.at[k, 0, 0], xto(1)).wait_send()
            part = dbuf.at[k, :, :, 0:32, :]
            rdma(part, part, dsem, down.at[k, 0], xto(1)).wait_send()

        @pl.when(root)
        def _():
            whole(rx.at[k, 1], dx.at[k, 1])

        @pl.when(nots(mate))
        def _():
            whole(rx.at[k, 2], dx.at[k, 2])

    for k in range(2):
        @pl.when(b == (r0, LAST)[k])
        def _():
            mine(k).wait()
    for m in own_h:
        m.wait()

    @pl.loop(1, 16)
    def _(i):
        rdma(hbuf.at[b], hbuf.at[b], hs.at[0], hr.at[0, i], partner).wait_send()
        rdma(piv, pbuf.at[b], hs.at[1], hr.at[1, i], partner).wait_send()


def comm(r0, cbuf, rbuf, loads, piv):
    anyspec = pl.BlockSpec(memory_space=pl.ANY)
    dma = pltpu.SemaphoreType.DMA
    return pl.pallas_call(
        functools.partial(comm_kernel, r0),
        out_shape=(
            jax.ShapeDtypeStruct(cbuf.shape, F32),
            jax.ShapeDtypeStruct(rbuf.shape, F32),
            jax.ShapeDtypeStruct((2, 2, 4, 64, W), F32),
            jax.ShapeDtypeStruct((16, 2, 1024), F32),
            jax.ShapeDtypeStruct((16, 2, 2 * W), F32),
        ),
        in_specs=[anyspec] * 4,
        out_specs=(anyspec,) * 5,
        input_output_aliases={0: 0, 1: 1},
        scratch_shapes=[
            dma((2, 4)), dma((2, 4)), dma((2, 4, N)),
            dma((2, 4)), dma((2, 3)), dma((2, 4, NR)), dma((2, 4)),
            dma((2, 4)), dma((2, 3)), dma((2, 4)), dma((2, 4)),
            dma((2,)), dma((2, 16)), dma((4,)),
        ],
        compiler_params=pltpu.CompilerParams(collective_id=r0, has_side_effects=True),
        name="exchange_%d" % r0,
    )(cbuf, rbuf, loads, piv)


def split(v):
    hi = v.astype(BF16)
    return hi, (v - hi.astype(F32)).astype(BF16)


def mm(a, b):
    return jnp.dot(a, b, preferred_element_type=F32)


def mm3(a, b):
    return mm(a[0], b[0]) + (mm(a[0], b[1]) + mm(a[1], b[0]))


def mm3t(a, b):
    dims = (((1,), (1,)), ((), ()))

    def one(p, q):
        return lax.dot_general(p, q, dims, preferred_element_type=F32)

    return one(a[0], b[0]) + (one(a[0], b[1]) + one(a[1], b[0]))


def full(a, b):
    return mm3(split(a), split(b))


def newton(pivot):
    n = pivot.shape[0]
    r = lax.broadcasted_iota(jnp.int32, (n, n), 0)
    c = lax.broadcasted_iota(jnp.int32, (n, n), 1)
    eye = r == c
    kept = jnp.where(eye, pivot, 0.0)
    drow = 1.0 / jnp.sum(kept, axis=0, keepdims=True)
    dcol = 1.0 / jnp.sum(kept, axis=1, keepdims=True)
    inv = jnp.where(eye, 2.0 * drow, 0.0) - dcol * (pivot * drow)
    for _ in range(NS_STEPS - 1):
        inv = 2.0 * inv - full(inv, full(pivot, inv))
    return inv


def update_kernel(weight, sc, fill, front, shift, cbuf, rbuf, dbuf, hbuf, pbuf, out, hout,
                  x0h, x0l, t1h, t1l, later, uh, ul, pvh, pvl, hs, weave):
    u = pl.program_id(0)
    s0, g, b = sc[0], lax.axis_index("grp"), lax.axis_index("blk")
    r0, q0 = s0 // 8, (s0 % 8) // 2
    cols = front.shape[1]
    ids = lax.broadcasted_iota(jnp.int32, (1, cols), 1) // W
    dead0 = (g == r0) & (ids == q0)
    dead1 = (g == LAST) & (ids == 3)

    @pl.when(u == 0)
    def _():
        d = [[dbuf[i, j].reshape(W, W) for j in range(2)] for i in range(2)]
        x0 = newton(d[0][0])
        m = full(d[1][0], x0)
        d11 = d[1][1] - full(m, d[0][1])
        x1 = newton(d11)
        x0h[...], x0l[...] = split(x0)
        t1h[0:W], t1l[0:W] = split(-full(full(x0, d[0][1]), x1))
        t1h[W : 2 * W], t1l[W : 2 * W] = split(x1)
        later[...] = d11
        ms = split(m)
        u0 = jnp.where(dead0, 0.0, rbuf[0])
        u0s = split(u0)
        u1 = jnp.where(dead0 | dead1, 0.0, rbuf[1] - mm3(ms, u0s))
        u1s = split(u1)
        uh[0:W], ul[0:W] = u0s
        uh[W : 2 * W], ul[W : 2 * W] = u1s
        pv = jnp.concatenate([pbuf[:, 0, :], pbuf[:, 1, :]], axis=0)
        p0 = split(pv[:, 0:W])
        p1 = split(pv[:, W : 2 * W] - mm3t(p0, ms))
        pvh[:, 0:W], pvl[:, 0:W] = p0
        pvh[:, W : 2 * W], pvl[:, W : 2 * W] = p1

    aq = quarter_of(u, s0, b)
    gone0 = (b == r0) & (aq == q0)
    gone1 = (b == LAST) & (aq == 3)
    c1 = cbuf[1].reshape(W, W)
    c0s, c1s = split(cbuf[0].reshape(W, W)), split(c1)
    both = tuple(jnp.concatenate([p, q], axis=1) for p, q in zip(c0s, c1s))
    l0 = jnp.where(gone0, 0.0, mm3(c0s, (x0h[...], x0l[...])))
    l1 = jnp.where(gone0 | gone1, 0.0, mm3(both, (t1h[...], t1l[...])))
    l0s, l1s = split(l0), split(l1)
    lh = jnp.concatenate([l0s[0], l1s[0]], axis=1)
    ll = jnp.concatenate([l0s[1], l1s[1]], axis=1)
    for j in range(cols // W):
        sl = slice(j * W, (j + 1) * W)
        f = masked(weight, front[:, sl], 2, 2, aq * 2, j * 2, fill, shift, g == b)
        f = f - mm3((lh, ll), (uh[:, sl], ul[:, sl]))
        f = jnp.where((g == r0) & (q0 == j) & jnp.logical_not(gone0), l0, f)
        if j == 3:
            f = jnp.where(g == LAST, jnp.where(gone0, c1, jnp.where(gone1, later[...], l1)), f)
        out[:, sl] = f
    here = pl.ds(pl.multiple_of(aq * W, W), W)
    h = jnp.concatenate([hbuf[:, 0, here], hbuf[:, 1, here]], axis=0)
    h = h - mm3t((pvh[...], pvl[...]), (lh, ll))
    hs[:, here] = h

    @pl.when(u == 3)
    def _():
        for j in range(cols // BS):
            lanes = slice(j * BS, (j + 1) * BS)
            weave[j, pl.ds(0, 16, stride=2), :] = hs[0:16, lanes]
            weave[j, pl.ds(1, 16, stride=2), :] = hs[16:32, lanes]
            hout[:, lanes] = weave[j]


def per_device(front, diag, fill, supernodes, loads):
    rows, cols = front.shape
    order = rows * lax.axis_size("blk")
    sc = supernodes
    weight = math.sqrt(order)
    shift = diag.reshape(rows // BS, BS)
    smem = pl.BlockSpec(memory_space=pltpu.SMEM)

    def const(shape):
        return pl.BlockSpec(shape, lambda u, sc: (0,) * len(shape))

    cbuf, rbuf, piv = pl.pallas_call(
        functools.partial(prep_kernel, weight),
        out_shape=(
            jax.ShapeDtypeStruct((2, 4, 256, W), F32),
            jax.ShapeDtypeStruct((2, W, cols), F32),
            jax.ShapeDtypeStruct((2, 2 * W), F32),
        ),
        grid_spec=pltpu.PrefetchScalarGridSpec(
            num_scalar_prefetch=1,
            grid=(4,),
            in_specs=[
                smem,
                pl.BlockSpec((W, W), lambda u, sc: (quarter_of(u, sc[0], lax.axis_index("blk")), (sc[0] % 8) // 2)),
                pl.BlockSpec((W, W), lambda u, sc: (quarter_of(u, sc[0], lax.axis_index("blk")), 3)),
                pl.BlockSpec((W, W), lambda u, sc: ((sc[0] % 8) // 2, u)),
                pl.BlockSpec((W, W), lambda u, sc: (3, u)),
                const(shift.shape),
                const(loads.shape),
            ],
            out_specs=(
                pl.BlockSpec((2, 4, 64, W), lambda u, sc: (0, 0, u, 0)),
                pl.BlockSpec((2, W, W), lambda u, sc: (0, 0, u)),
                const((2, 2 * W)),
            ),
        ),
        name="panels",
    )(sc, fill, front, front, front, front, shift, loads)
    rbuf = rbuf.reshape(2, 2, 4, 32, cols)
    cbuf, rbuf, dbuf, hbuf, pbuf = lax.switch(
        supernodes[0] // 8, [functools.partial(comm, r) for r in range(16)], cbuf, rbuf, loads, piv)
    rbuf = rbuf.reshape(2, W, cols)
    out, hout = pl.pallas_call(
        functools.partial(update_kernel, weight),
        out_shape=(
            jax.ShapeDtypeStruct((rows, cols), F32),
            jax.ShapeDtypeStruct((32, rows), F32),
        ),
        grid_spec=pltpu.PrefetchScalarGridSpec(
            num_scalar_prefetch=1,
            grid=(4,),
            in_specs=[
                smem,
                pl.BlockSpec((W, cols), lambda u, sc: (quarter_of(u, sc[0], lax.axis_index("blk")), 0)),
                const(shift.shape),
                pl.BlockSpec((2, 4, 64, W), lambda u, sc: (0, 0, u, 0)),
                const(rbuf.shape),
                const(dbuf.shape),
                const(hbuf.shape),
                const(pbuf.shape),
            ],
            out_specs=(
                pl.BlockSpec((W, cols), lambda u, sc: (quarter_of(u, sc[0], lax.axis_index("blk")), 0)),
                const((32, rows)),
            ),
            scratch_shapes=[pltpu.VMEM((W, W), BF16)] * 2
            + [pltpu.VMEM((2 * W, W), BF16)] * 2
            + [pltpu.VMEM((W, W), F32)]
            + [pltpu.VMEM((2 * W, cols), BF16)] * 2
            + [pltpu.VMEM((32, 2 * W), BF16)] * 2
            + [pltpu.VMEM((32, rows), F32), pltpu.VMEM((rows // BS, 32, BS), F32)],
        ),
        name="update",
    )(sc, fill, front, shift, cbuf, rbuf, dbuf, hbuf, pbuf)
    return out, hout


def solution(mesh):
    in_specs = (P("blk", "grp"), P("blk"), P("blk", "grp"), P(), P(("grp", "blk"), None))
    out_specs = (P("blk", "grp"), P("grp", "blk"))
    return jax.shard_map(
        per_device, mesh=mesh, in_specs=in_specs, out_specs=out_specs, check_vma=False
    )
```
